256 devices in a mesh: seq: 4 (over x), batch: 16 (over z, core), mp: 4 (over y).
Axes of the slice: x: 4, y: 4, z: 8, core: 2. Of those that a mesh axis runs over, the one named last changes fastest.
Arguments:
- xs: bfloat16 [16, 1536, 8192], P('batch', 'seq', 'mp'), may hold values from -6 to 6
- gate_z: bfloat16 [16, 1536, 8192], P('batch', 'seq', 'mp'), may hold values from -16 to 16
- b_in: bfloat16 [16, 1536, 128], P('batch', 'seq'), may hold values from -1.796875 to 1.796875
- c_in: bfloat16 [16, 1536, 128], P('batch', 'seq'), may hold values from -1.796875 to 1.796875
- log_decay: float32 [16, 1536, 128], P('batch', 'seq', 'mp'), may hold values from -4 to 0
- d_skip: float32 [128], P('mp'), may hold values from 0.5 to 2
- norm_gain: float32 [8192], P('mp'), may hold values from 0.5 to 1.5
- queries: bfloat16 [16, 1536, 4096], P('batch', 'seq', 'mp'), may hold values from -6 to 6
- keys_new: bfloat16 [16, 1536, 1024], P('batch', 'seq', 'mp'), may hold values from -6 to 6
- values_new: bfloat16 [16, 1536, 1024], P('batch', 'seq', 'mp'), may hold values from -6 to 6
- kv_pool: bfloat16 [512, 2, 64, 1024], P('batch', None, None, 'mp'), may hold values from -6 to 6
- state_pool: bfloat16 [1024, 128, 2, 128], P('batch', 'mp'), may hold values from -6 to 6
- new_len: int32 [16], P('batch'), may hold values from 384 to 1536, as said below
- cached_blocks: int32 [16], P('batch'), may hold values from 1 to 32, 384 in all
- kv_owner: int32 [16, 32, 1], P('batch'), may hold values from 0 to 15; in each aligned block of 32 rows (0 to 31, 32 to 63, ..., all dimensions but the last counted through in order) at most 3 rows name the same one
- kv_slot: int32 [16, 32], P('batch'), may hold values from 0 to 31
- state_owner: int32 [16, 32, 1], P('batch'), may hold values from 0 to 15; in each aligned block of 32 rows (0 to 31, 32 to 63, ..., all dimensions but the last counted through in order) at most 3 rows name the same one
- state_slot: int32 [16, 32], P('batch'), may hold values from 0 to 63
Outputs:
- ssm_out: bfloat16 [16, 1536, 8192], P('batch', 'seq', 'mp')
- attn_out: bfloat16 [16, 1536, 4096], P('batch', 'seq', 'mp')
The draws below stay inside these ranges and needn't reach their ends.
Inputs may be any that keep to these rules, and one draw needn't show every extreme that they name: `new_len`: at least 384; some prompt has exactly 1536. `kv_owner`: among the 32 entries of one prompt's list no owner appears more than 3 times. `state_owner`: among the 32 pieces of one prompt no owner appears more than 3 times.
All inputs are finite; a program needn't handle non-finite values. No bound on the sum of `cached_blocks` on one device may be relied on, other than what follows from the above.
Results may differ from the reference program's by a relative error of at most 0.0085.
Values may be sent and summed in bfloat16 or wider, within the bound.
A program may use at most 128 MiB of HBM per device.

```python
import math
import jax
import jax.numpy as jnp
import numpy as np
from jax import lax

STRETCH = 384
H = 128
P_SIZE = 64
N = 128
QH = 32
KVH = 8
HD = 128
BQ = 128
BLK = 64
POOL_DEV = 32
SPOOL_DEV = 64
PROMPT_COUNT = 16
NEW_TOKEN_SLOTS = 1536
MAXB = 32
CAP = 3
SPIECES = 32
PP = 2
POOL_ALL = 512
SPOOL_ALL = 1024
N_BATCH = 16


def draw_new_len(key, part):
    first_key, second_key = jax.random.split(jax.random.fold_in(key, 3))
    extra = jax.random.randint(first_key, (PROMPT_COUNT,), 0, 3 * STRETCH + 1)
    longest = jax.random.randint(second_key, (), 0, PROMPT_COUNT)
    lengths_all = STRETCH + extra
    return jnp.where(jnp.arange(PROMPT_COUNT) == longest, NEW_TOKEN_SLOTS, lengths_all).astype(jnp.int32)


def draw_log_decay(key, part):
    every_key_row = jax.random.split(jax.random.fold_in(key, 5), 7)
    slow_share = 0.5
    slow_heads = jax.random.uniform(every_key_row[0], (H,)) < slow_share
    slow_rate = jnp.exp(jax.random.uniform(every_key_row[1], (H,), minval=math.log(1.0 / (8.0 * NEW_TOKEN_SLOTS)), maxval=math.log(1.0 / (3.0 * NEW_TOKEN_SLOTS))))
    quick_rate = jnp.exp(jax.random.uniform(every_key_row[2], (H,), minval=math.log(1.0 / 400.0), maxval=math.log(1.0 / 30.0)))
    rates = jnp.where(slow_heads, slow_rate, quick_rate)
    per_prompt = jnp.exp(jax.random.uniform(every_key_row[3], (PROMPT_COUNT, 1, 1), minval=math.log(0.5), maxval=math.log(2.0)))
    jitter = jnp.exp(jax.random.uniform(every_key_row[4], (PROMPT_COUNT, NEW_TOKEN_SLOTS, H), minval=math.log(0.5), maxval=math.log(2.0)))
    token_runs = jax.random.randint(every_key_row[5], (PROMPT_COUNT, 3), 0, NEW_TOKEN_SLOTS)
    masked_out_flags = jnp.any(jnp.arange(NEW_TOKEN_SLOTS)[None, :, None] == token_runs[:, None, :], axis=-1)
    losses = jax.random.uniform(every_key_row[6], (PROMPT_COUNT, NEW_TOKEN_SLOTS, H), minval=math.log(0.5), maxval=math.log(0.8))
    values_all = -rates[None, None, :] * per_prompt * jitter + jnp.where(masked_out_flags[:, :, None], losses, 0.0)
    return jnp.clip(values_all, -4.0, 0.0).astype(jnp.float32)


def draw_gate_z(key, part):
    first_key, second_key, third_key = jax.random.split(jax.random.fold_in(key, 11), 3)
    channels = H * P_SIZE
    ramp = jnp.exp(math.log(3.0) * jnp.arange(channels, dtype=jnp.float32) / channels)
    column_scale = jnp.exp(jax.random.uniform(first_key, (channels,), minval=0.0, maxval=math.log(4.0)))
    row_scale = jnp.exp(jax.random.uniform(second_key, (PROMPT_COUNT, NEW_TOKEN_SLOTS, 1), minval=0.0, maxval=math.log(10.0)))
    base = jax.random.normal(third_key, (PROMPT_COUNT, NEW_TOKEN_SLOTS, channels))
    return jnp.clip(0.15 * base * ramp * column_scale * row_scale, -16.0, 16.0).astype(jnp.bfloat16)


def drawn_pair(key):
    base_key = jax.random.fold_in(key, 17)
    query_key, fresh_key = jax.random.split(base_key, 2)
    group = QH // KVH
    query_all = jax.random.normal(query_key, (PROMPT_COUNT, NEW_TOKEN_SLOTS, KVH, group, HD))
    fresh_all = jax.random.normal(fresh_key, (PROMPT_COUNT, NEW_TOKEN_SLOTS, KVH, HD))
    query_all = jnp.clip(query_all, -6.0, 6.0).reshape(PROMPT_COUNT, NEW_TOKEN_SLOTS, QH * HD)
    fresh_all = jnp.clip(fresh_all, -6.0, 6.0).reshape(PROMPT_COUNT, NEW_TOKEN_SLOTS, KVH * HD)
    return (query_all, fresh_all)


def draw_queries(key, part):
    return drawn_pair(key)[0].astype(jnp.bfloat16)


def draw_keys_new(key, part):
    return drawn_pair(key)[1].astype(jnp.bfloat16)


def set_ends(values, stream_key, smallest, largest):
    longest = values.shape.index(max(values.shape))
    spots = []
    for shift in (0, 1):
        where = [jax.random.randint(jax.random.fold_in(stream_key, axis), (), 0, length) for axis, length in enumerate(values.shape)]
        where[longest] = (where[longest] + shift) % values.shape[longest]
        spots.append(tuple(where))
    return values.at[spots[0]].set(smallest).at[spots[1]].set(largest)


def shard_levels(key, extent, shards, smallest, high):
    gain = 1.0
    for dim, blocks in shards:
        heights = jax.random.uniform(jax.random.fold_in(jax.random.fold_in(key, 6), dim), (blocks,), jnp.float32, smallest / len(shards), high / len(shards))
        gain = gain * jnp.repeat(jnp.exp(heights), extent[dim] // blocks).reshape((-1,) + (1,) * (len(extent) - 1 - dim))
    return gain


def profile(amount, total, limit, lean):
    weights = [(1 << 20) // math.isqrt(standing ** lean) + 1 for standing in range(2, amount + 1)]
    rest, holding = total - limit - (amount - 1), [1] * (amount - 1)
    while rest > 0:
        movable = [i for i in range(amount - 1) if holding[i] < limit]
        pool, left = sum([weights[i] for i in movable]), rest
        for i in movable:
            more = min(limit - holding[i], max(1, left * weights[i] // pool), rest)
            holding[i] = holding[i] + more
            rest = rest - more
    return np.array([limit] + holding)


def ragged(stream_key, amount, total, limit, slope):
    if amount == 2:
        one = jax.random.randint(stream_key, (), max(1, total - limit), min(limit, total - 1) + 1)
        return jnp.stack([one, total - one])
    sizes = jnp.asarray(profile(amount, total, limit, slope), jnp.int32)
    pairs = (amount - 1) // 2
    source_of, taker = sizes[1:1 + 2 * pairs:2], sizes[2:2 + 2 * pairs:2]
    room = jnp.minimum(source_of - 1, limit - taker)
    moved = jax.random.randint(jax.random.fold_in(stream_key, 1), (pairs,), 0, 1 << 20) % (room + 1)
    sizes = sizes.at[1:1 + 2 * pairs:2].set(source_of - moved).at[2:2 + 2 * pairs:2].set(taker + moved)
    return sizes[jax.random.permutation(jax.random.fold_in(stream_key, 2), amount)]


def routed_block(own_key, own, number, rows, count, top, bound, slope):
    sequence = jax.random.permutation(own_key, count)
    packed, ordinary = shares(count, rows * top, bound, slope, True), shares(count, rows * top, bound, slope, False)
    places = jnp.arange(count)

    def named(tallies, rotation):
        used = int((tallies > 0).sum())
        fixed = max(1, used // 4)
        moved = fixed + (places - fixed + rotation * (used - fixed)) % max(1, count - fixed)
        return jnp.zeros((count,), jnp.int32).at[sequence[jnp.where(places < fixed, places, moved)]].set(jnp.asarray(tallies, jnp.int32))

    tallies = jnp.where(number % 4 == 0, named(packed, number // 4), named(ordinary, number - number // 4 - 1))
    mixed = jax.random.permutation(jax.random.fold_in(own, 3), count)
    donor, taker = mixed[0:count // 2 * 2:2], mixed[1:count // 2 * 2:2]
    room = jnp.minimum(tallies[donor] - 1, bound - tallies[taker]) // 2
    room = jnp.where((donor == sequence[0]) | (taker == sequence[0]) | (tallies[taker] == 0), 0, jnp.maximum(room, 0))
    moved = jax.random.randint(jax.random.fold_in(own, 4), (count // 2,), 0, 1 << 20) % (room + 1)
    tallies = tallies.at[donor].add(-moved).at[taker].add(moved)
    members = jnp.searchsorted(jnp.cumsum(tallies), jnp.arange(rows * top), side="right").astype(jnp.int32)
    table = members.reshape(top, rows).T
    table = table[jax.random.permutation(jax.random.fold_in(own, 1), rows)]
    rotation = jax.random.randint(jax.random.fold_in(own, 2), (rows, 1), 0, top)
    return jnp.take_along_axis(table, (jnp.arange(top)[None, :] + rotation) % top, axis=1)


def shares(amount, total, bound, lean, full):
    portions = [(1 << 20) // math.isqrt(rank ** lean) + 1 for rank in range(1, amount + 1)]
    largest = bound if full else min(bound, max(-(-total // amount), total * portions[0] // sum(portions)))
    least = 1 if total - largest >= amount - 1 else 0
    counts, rest = [largest] + [least] * (amount - 1), total - largest - least * (amount - 1)
    while rest > 0:
        movable = [i for i in range(1, amount) if counts[i] < largest] or [i for i in range(1, amount) if counts[i] < bound]
        pool, left = sum([portions[i] for i in movable]), rest
        for i in movable:
            more = min(bound - counts[i], max(1, left * portions[i] // pool), rest)
            counts[i] = counts[i] + more
            rest = rest - more
    return np.array(counts)


def noise(rng, extent, deviation, reach, shards=(), kind=jnp.bfloat16):
    array = jax.random.normal(rng, extent, jnp.float32) * deviation
    if len(shards) > 0:
        array = shard_levels(rng, extent, shards, -0.22, 0.18) * array
    return jnp.clip(array, min=-reach, max=reach).astype(kind)


def setup_inputs(seed: int = 0) -> dict:
    seeds = jax.random.split(jax.random.key(seed), 19)
    xs = noise(seeds[0], (PROMPT_COUNT, NEW_TOKEN_SLOTS, H * P_SIZE), 1.0, 6.0, ((0, 16), (1, 4), (2, 4)))
    gate_z = draw_gate_z(jax.random.fold_in(seeds[18], 71), 0)
    b_in = noise(seeds[2], (PROMPT_COUNT, NEW_TOKEN_SLOTS, N), 0.3, 1.796875, ((0, 16), (1, 4)))
    c_in = noise(seeds[3], (PROMPT_COUNT, NEW_TOKEN_SLOTS, N), 0.3, 1.796875, ((0, 16), (1, 4)))
    log_decay = draw_log_decay(jax.random.fold_in(seeds[18], 71), 0)
    d_skip = jnp.clip(jnp.exp(math.log(2.0) - 1.3862944 * jax.random.uniform(seeds[5], (H,), jnp.float32) ** shard_levels(seeds[5], (H,), ((0, 4),), -0.2, 0.2)), 0.5, 2.0)
    norm_gain = jnp.clip(1.0 + 0.1 * jax.random.normal(seeds[6], (H * P_SIZE,), jnp.float32), 0.5, 1.5)
    queries = draw_queries(jax.random.fold_in(seeds[18], 71), 0)
    keys_new = draw_keys_new(jax.random.fold_in(seeds[18], 71), 0)
    values_new = noise(seeds[9], (PROMPT_COUNT, NEW_TOKEN_SLOTS, KVH * HD), 1.0, 6.0, ((0, 16), (1, 4), (2, 4)))
    kv_pool = noise(seeds[10], (POOL_ALL, 2, BLK, KVH * HD), 1.0, 6.0, ((0, 16), (3, 4)))
    state_pool = noise(seeds[11], (SPOOL_ALL, H, PP, N), 1.0, 6.0, ((0, 16), (1, 4)))
    new_len = draw_new_len(jax.random.fold_in(seeds[18], 71), 0)
    cached_blocks = ragged(seeds[13], PROMPT_COUNT, PROMPT_COUNT * MAXB * 3 // 4, MAXB, 2).astype(jnp.int32)
    kv_owner_keys = jax.random.split(jax.random.fold_in(seeds[14], 1), PROMPT_COUNT * MAXB // MAXB)
    kv_owner_turns = jax.random.permutation(jax.random.fold_in(seeds[14], 3), PROMPT_COUNT * MAXB // MAXB)
    kv_owner = jax.vmap(lambda own, number: routed_block(jax.random.fold_in(seeds[14], 2), own, number, MAXB, N_BATCH, 1, CAP, 2))(kv_owner_keys, kv_owner_turns).reshape((PROMPT_COUNT, MAXB, 1))
    kv_slot = set_ends(jax.random.randint(seeds[15], (PROMPT_COUNT, MAXB), 0, POOL_DEV), jax.random.fold_in(seeds[15], 1), 0, POOL_DEV - 1).astype(jnp.int32)
    state_owner_keys = jax.random.split(jax.random.fold_in(seeds[16], 1), PROMPT_COUNT * SPIECES // SPIECES)
    state_owner_turns = jax.random.permutation(jax.random.fold_in(seeds[16], 3), PROMPT_COUNT * SPIECES // SPIECES)
    state_owner = jax.vmap(lambda own, number: routed_block(jax.random.fold_in(seeds[16], 2), own, number, SPIECES, N_BATCH, 1, CAP, 1))(state_owner_keys, state_owner_turns).reshape((PROMPT_COUNT, SPIECES, 1))
    state_slot = set_ends(jax.random.randint(seeds[17], (PROMPT_COUNT, SPIECES), 0, SPOOL_DEV), jax.random.fold_in(seeds[17], 1), 0, SPOOL_DEV - 1).astype(jnp.int32)
    return dict(xs=xs, gate_z=gate_z, b_in=b_in, c_in=c_in, log_decay=log_decay, d_skip=d_skip, norm_gain=norm_gain, queries=queries, keys_new=keys_new, values_new=values_new, kv_pool=kv_pool, state_pool=state_pool, new_len=new_len, cached_blocks=cached_blocks, kv_owner=kv_owner, kv_slot=kv_slot, state_owner=state_owner, state_slot=state_slot)


PRECISE = lax.Precision.HIGHEST
EPSILON = 1e-05
NEGATIVE = -1e+30

def block_scan(state_in, inputs_x, inputs_b, inputs_c, decay_part):
    running = jnp.cumsum(decay_part, axis=0)
    span_here = decay_part.shape[0]
    lower = jnp.arange(span_here)[:, None] >= jnp.arange(span_here)[None, :]
    spread = running.T[:, :, None] - running.T[:, None, :]
    factors = jnp.where(lower[None], jnp.exp(jnp.minimum(spread, 0.0)), 0.0)
    intersections = jnp.dot(inputs_c, inputs_b.T, precision=PRECISE)
    inner = jnp.einsum('hts,shp->thp', factors * intersections[None], inputs_x, precision=PRECISE)
    carried = jnp.einsum('tn,hpn->thp', inputs_c, state_in, precision=PRECISE) * jnp.exp(running)[:, :, None]
    remain = jnp.exp(running[-1][None, :] - running)
    state_out = jnp.exp(running[-1])[:, None, None] * state_in + jnp.einsum('shp,sn->hpn', inputs_x * remain[:, :, None], inputs_b, precision=PRECISE)
    return (state_out, inner + carried)

def reference(xs, gate_z, b_in, c_in, log_decay, d_skip, norm_gain, queries, keys_new, values_new, kv_pool, state_pool, new_len, cached_blocks, kv_owner, kv_slot, state_owner, state_slot):

    def ssm_prompt(bundle):
        inputs, gates, inputs_b, inputs_c, decays, prompt_len, owners, slots = bundle
        valid = (jnp.arange(NEW_TOKEN_SLOTS) < prompt_len).astype(jnp.float32)
        inputs_x = inputs.astype(jnp.float32).reshape(NEW_TOKEN_SLOTS, H, P_SIZE) * valid[:, None, None]
        decay_in = decays * valid[:, None]
        pieces = state_pool[owners * SPOOL_DEV + slots]
        start_state = jnp.transpose(pieces, (1, 0, 2, 3)).reshape(H, P_SIZE, N).astype(jnp.float32)
        block_count = NEW_TOKEN_SLOTS // BQ

        def advance(state, blocked):
            return block_scan(state, blocked[0], blocked[1], blocked[2], blocked[3])
        blocked_all = (inputs_x.reshape(block_count, BQ, H, P_SIZE), inputs_b.astype(jnp.float32).reshape(block_count, BQ, N), inputs_c.astype(jnp.float32).reshape(block_count, BQ, N), decay_in.reshape(block_count, BQ, H))
        unused, outputs = lax.scan(advance, start_state, blocked_all)
        scan_out = outputs.reshape(NEW_TOKEN_SLOTS, H, P_SIZE) + d_skip[None, :, None] * inputs_x
        gated = scan_out * jax.nn.silu(gates.astype(jnp.float32).reshape(NEW_TOKEN_SLOTS, H, P_SIZE))
        square_mean = lax.optimization_barrier(jnp.sum(gated * gated, axis=(1, 2))) / (H * P_SIZE)
        normed = gated * lax.rsqrt(square_mean + EPSILON)[:, None, None] * norm_gain.reshape(H, P_SIZE)
        return (normed * valid[:, None, None]).reshape(NEW_TOKEN_SLOTS, H * P_SIZE).astype(jnp.bfloat16)

    def attention_prompt(bundle):
        query_all, key_fresh, value_fresh, prompt_len, block_total, owners, slots = bundle
        records = kv_pool[owners * POOL_DEV + slots]
        cached_keys = records[:, 0].reshape(MAXB * BLK, KVH, HD)
        cached_values = records[:, 1].reshape(MAXB * BLK, KVH, HD)
        all_keys = jnp.concatenate([cached_keys, key_fresh.reshape(NEW_TOKEN_SLOTS, KVH, HD)], axis=0).astype(jnp.float32)
        all_values = jnp.concatenate([cached_values, value_fresh.reshape(NEW_TOKEN_SLOTS, KVH, HD)], axis=0).astype(jnp.float32)
        cached_usable = jnp.arange(MAXB * BLK) // BLK < block_total
        fresh_pos = jnp.arange(NEW_TOKEN_SLOTS)
        fresh_usable = fresh_pos < prompt_len
        query_blocks = query_all.reshape(NEW_TOKEN_SLOTS // STRETCH, STRETCH, KVH, QH // KVH, HD)

        def query_block(bundle_inner):
            block_queries, start = bundle_inner
            query_pos = start + jnp.arange(STRETCH)
            causal = (fresh_pos[None, :] <= query_pos[:, None]) & fresh_usable[None, :]
            allowed = jnp.concatenate([jnp.broadcast_to(cached_usable[None, :], (STRETCH, MAXB * BLK)), causal], axis=1)
            scores = jnp.einsum('tkgd,skd->kgts', block_queries.astype(jnp.float32), all_keys, precision=PRECISE) * HD ** (-0.5)
            scores = jnp.where(allowed[None, None], scores, NEGATIVE)
            highest = lax.optimization_barrier(jnp.max(scores, axis=-1, keepdims=True))
            probs = jnp.where(allowed[None, None], jnp.exp(scores - highest), 0.0)
            denominator = lax.optimization_barrier(jnp.sum(probs, axis=-1))
            rounded = lax.optimization_barrier(probs.astype(jnp.bfloat16))
            weights = rounded.astype(jnp.float32)
            numerator = jnp.einsum('kgts,skd->kgtd', weights, all_values, precision=PRECISE)
            result = numerator / denominator[..., None]
            result = jnp.transpose(result, (2, 0, 1, 3)).reshape(STRETCH, QH * HD)
            query_valid = (query_pos < prompt_len).astype(jnp.float32)
            return (result * query_valid[:, None]).astype(jnp.bfloat16)
        starts = (jnp.arange(NEW_TOKEN_SLOTS // STRETCH) * STRETCH).astype(jnp.int32)
        return lax.map(query_block, (query_blocks, starts)).reshape(NEW_TOKEN_SLOTS, QH * HD)
    ssm_out = lax.map(ssm_prompt, (xs, gate_z, b_in, c_in, log_decay, new_len, state_owner[:, :, 0], state_slot))
    attn_out = lax.map(attention_prompt, (queries, keys_new, values_new, new_len, cached_blocks, kv_owner[:, :, 0], kv_slot))
    return (ssm_out, attn_out)
```

```python
import functools

import jax
import jax.numpy as jnp
from jax import lax
from jax.experimental import pallas as pl
from jax.experimental.pallas import tpu as pltpu
from jax.sharding import PartitionSpec as P

T = 384
CH = 2048
HEADS = 32
NS = 128
BQ = 128
NCH = T // BQ
CAP = 3
OWN = 16
SEQ = 4
MPS = 4
ENT = 32
QH = 8
HD = 128
KEYS = 512
LT = 256
EPSILON = 1e-05
NEGATIVE = -1e30
LOG2E = 1.4426950408889634
SCALE2 = HD ** (-0.5) * LOG2E
MESH = pl.DeviceIdType.MESH
F32, BF16, I32 = jnp.float32, jnp.bfloat16, jnp.int32


def iota(shape, dim):
    return lax.broadcasted_iota(I32, shape, dim)


def dot(a, b, dims=((1,), (0,)), precision=None):
    return lax.dot_general(
        a, b, (dims, ((), ())), precision=precision, preferred_element_type=F32
    )


def high_low(v):
    high = v.astype(BF16)
    return jnp.concatenate([high, (v - high.astype(F32)).astype(BF16)], axis=1)


def ranks_of(owner):
    lane, row = iota((ENT, 128), 1), iota((ENT, 128), 0)
    column = jnp.sum(jnp.where(lane == row, owner, 0), axis=1, keepdims=True)
    same = (column == owner) & (row < lane)
    return jnp.sum(jnp.where(same, 1, 0), axis=0, keepdims=True)


def kernel(
    new_len, cached, meta, b_ref, c_ref, ld_ref, dsk_ref, gain_ref,
    x_hbm, z_hbm, q_hbm, k_hbm, v_hbm, kvp_hbm, stp_hbm,
    ssm_ref, attn_ref,
    x_v, z_v, q_v, nkv, kvq, stq, tab_v, rtab_v, pos_v, rtab_s, pos_s,
    skv, rk, rv, kvall, sst, rst, sta, sts, inc, snd, ssx,
    cum_v, cumt_v, ecx_v, e2_v, thr_v, g_v, bt_v, rem_v, l_v, lend_v, y_v, m_v, acc_v,
    load_sem, tab_sem, z_sem, st_sem, ag_sem, nk_sem, sx_sem, ch_sem, mp_sem,
):
    arrived = (rk, rv)
    s, b, m = lax.axis_index("seq"), lax.axis_index("batch"), lax.axis_index("mp")

    quarter = pl.ds(pl.multiple_of(s * 16, 16), 16)
    loads = [
        pltpu.make_async_copy(stp_hbm.at[:, quarter, :], stq, load_sem.at[0]),
        pltpu.make_async_copy(kvp_hbm.at[:, :, quarter, :], kvq, load_sem.at[1]),
        pltpu.make_async_copy(k_hbm, nkv.at[s, 0], load_sem.at[2]),
        pltpu.make_async_copy(v_hbm, nkv.at[s, 1], load_sem.at[3]),
        pltpu.make_async_copy(x_hbm, x_v, load_sem.at[4]),
        pltpu.make_async_copy(q_hbm, q_v, load_sem.at[5]),
        pltpu.make_async_copy(z_hbm, z_v, load_sem.at[6]),
    ]
    for load in loads:
        load.start()

    barrier = pltpu.get_barrier_semaphore()

    def greet(d, _):
        pl.semaphore_signal(barrier, inc=1, device_id=(s, lax.rem(b + d, OWN), m), device_id_type=MESH)
        return 0

    lax.fori_loop(1, OWN, greet, 0)
    for d in range(1, SEQ):
        pl.semaphore_signal(barrier, inc=1, device_id=(lax.rem(s + d, SEQ), b, m), device_id_type=MESH)
    for d in range(1, MPS):
        pl.semaphore_signal(barrier, inc=1, device_id=(s, b, lax.rem(m + d, MPS)), device_id_type=MESH)

    lists = meta[...]
    lane16, row16 = iota((OWN, 128), 1), iota((OWN, 128), 0)
    table = jnp.zeros((OWN, 128), I32)
    for part in range(2):
        owner, slot = lists[2 * part : 2 * part + 1], lists[2 * part + 1 : 2 * part + 2]
        rank = ranks_of(owner)
        pos_v[part : part + 1, :] = jnp.clip(owner * CAP + rank, 0, OWN * CAP - 1)
        for c in range(CAP):
            hit = (owner == row16) & (rank == c) & (lane16 < ENT)
            asked = jnp.sum(jnp.where(hit, slot, 0), axis=1, keepdims=True)
            table = jnp.where(lane16 == part * CAP + c, asked, table)
    for o in range(OWN):
        tab_v[o] = table[o : o + 1]
    rtab_v[b] = tab_v[b]
    to_pos = pltpu.make_async_copy(pos_v, pos_s, load_sem.at[7])
    to_pos.start()

    pl.semaphore_wait(barrier, OWN - 1 + SEQ - 1 + MPS - 1)

    def tab_copy(d):
        peer = lax.rem(b + d, OWN)
        return pltpu.make_async_remote_copy(
            src_ref=tab_v.at[peer], dst_ref=rtab_v.at[b], send_sem=tab_sem.at[0, d], recv_sem=tab_sem.at[1, d],
            device_id=(s, peer, m), device_id_type=MESH)

    def tab_from(d):
        source = lax.rem(b + OWN - d, OWN)
        return pltpu.make_async_remote_copy(
            src_ref=tab_v.at[source], dst_ref=rtab_v.at[source], send_sem=tab_sem.at[0, d], recv_sem=tab_sem.at[1, d],
            device_id=(s, source, m), device_id_type=MESH)

    def st_copy(d, to):
        peer = lax.rem(b + d, OWN) if to else lax.rem(b + OWN - d, OWN)
        at = b if to else peer
        return pltpu.make_async_remote_copy(
            src_ref=sst.at[pl.ds(peer * CAP, CAP)], dst_ref=rst.at[pl.ds(at * CAP, CAP)],
            send_sem=st_sem.at[0, d], recv_sem=st_sem.at[1, d], device_id=(s, peer, m), device_id_type=MESH)

    def kv_copy(part, d, to):
        peer = lax.rem(b + d, OWN) if to else lax.rem(b + OWN - d, OWN)
        at = b if to else peer
        return pltpu.make_async_remote_copy(
            src_ref=skv.at[part, pl.ds(peer * CAP, CAP)], dst_ref=arrived[part].at[pl.ds(at * CAP, CAP)],
            send_sem=z_sem.at[0, part, d], recv_sem=z_sem.at[1, part, d], device_id=(s, peer, m), device_id_type=MESH)

    def each_peer(act):
        def one(d, _):
            act(d)
            return 0

        lax.fori_loop(1, OWN, one, 0)

    each_peer(lambda d: tab_copy(d).start())

    loads[2].wait()
    loads[3].wait()

    def nk_copy(d, to):
        other = lax.rem(s + d, SEQ) if to else lax.rem(s + SEQ - d, SEQ)
        at = s if to else other
        return pltpu.make_async_remote_copy(
            src_ref=nkv.at[at], dst_ref=nkv.at[at], send_sem=nk_sem.at[0, d], recv_sem=nk_sem.at[1, d],
            device_id=(other, b, m), device_id_type=MESH)

    for d in range(1, SEQ):
        @pl.when(s + d < SEQ)
        def _(d=d):
            nk_copy(d, True).start()

    tri = jnp.where(iota((BQ, BQ), 0) >= iota((BQ, BQ), 1), 1.0, 0.0)
    triu = jnp.where(iota((BQ, BQ), 0) <= iota((BQ, BQ), 1), 1.0, 0.0)
    valid = jnp.where(s * T + iota((T, 1), 0) < new_len[0], 1.0, 0.0)
    e2_v[...] = jnp.where((iota((2 * HEADS, CH), 0) & (HEADS - 1)) == (iota((2 * HEADS, CH), 1) >> 6), 1.0, 0.0).astype(BF16)
    totals = []
    for k in range(NCH):
        rows = slice(k * BQ, (k + 1) * BQ)
        dec = ld_ref[rows, :] * valid[rows]
        cum = dot(tri, dec, precision=lax.Precision.HIGHEST)
        cumt_v[k * HEADS : (k + 1) * HEADS, :] = LOG2E * dot(dec, triu, ((0,), (0,)), lax.Precision.HIGHEST)
        cum_v[rows, :] = LOG2E * cum
        total = cum[BQ - 1 : BQ]
        totals.append(total)
        ecx_v[rows, :] = high_low(jnp.exp(cum))
        rem_v[rows, :] = high_low(jnp.exp(total - cum) * valid[rows])
        bt_v[:, rows] = b_ref[rows, :].astype(F32).T.astype(BF16)
        g = dot(c_ref[rows, :], b_ref[rows, :], ((1,), (1,)))
        g_v[k] = g * tri
    row = iota((16, HEADS), 0)
    small = jnp.where(row == 3, jnp.exp(totals[0] + totals[1] + totals[2]), jnp.where(row == 4, dsk_ref[...], 0.0))
    for k in range(NCH):
        small = jnp.where(row == k, jnp.exp(totals[k]), small)
    thr_v[...] = dot(high_low(small), e2_v[...])

    each_peer(lambda d: tab_from(d).wait_recv())
    to_tab = pltpu.make_async_copy(rtab_v, rtab_s, load_sem.at[8])
    to_tab.start()
    to_tab.wait()
    to_pos.wait()
    loads[0].wait()

    def pack_state(i, _):
        for c in range(CAP):
            sst[i * CAP + c] = stq[jnp.clip(rtab_s[i, 0, CAP + c], 0, 63)]
        return 0

    lax.fori_loop(0, OWN, pack_state, 0)
    each_peer(lambda d: st_copy(d, True).start())
    loads[1].wait()
    for part in range(2):
        def pack_kv(i, _, part=part):
            for c in range(CAP):
                skv[part, i * CAP + c] = kvq[jnp.clip(rtab_s[i, 0, c], 0, 31), part]
            return 0

        lax.fori_loop(0, OWN, pack_kv, 0)
        each_peer(lambda d, part=part: kv_copy(part, d, True).start())
    for c in range(CAP):
        rst[b * CAP + c] = sst[b * CAP + c]
        for part in range(2):
            arrived[part][b * CAP + c] = skv[part, b * CAP + c]

    loads[4].wait()

    def end_tile(j, _):
        lanes = pl.ds(pl.multiple_of(j * LT, LT), LT)
        total = None
        for k in range(NCH):
            rows = slice(k * BQ, (k + 1) * BQ)
            xr = (x_v[rows, lanes].astype(F32) * dot(rem_v[rows, :], e2_v[:, lanes])).astype(BF16)
            part = dot(bt_v[:, rows], xr)
            if k < NCH - 1:
                l_v[k, :, lanes] = part
            total = part if k == 0 else thr_v[k : k + 1, lanes] * total + part
        lend_v[:, lanes] = total
        return 0

    lax.fori_loop(0, CH // LT, end_tile, 0)

    each_peer(lambda d: st_copy(d, False).wait_recv())

    def place(j, _):
        sta[pl.ds(pl.multiple_of(j * 16, 16), 16), :] = rst[jnp.clip(pos_s[1, j], 0, OWN * CAP - 1)]
        return 0

    lax.fori_loop(0, ENT, place, 0)
    r, c = iota((KEYS, KEYS), 0), iota((KEYS, KEYS), 1)
    order = jnp.where(c == ((r >> 1) & 7) * 64 + (r >> 4) * 2 + (r & 1), 1.0, 0.0).astype(BF16)
    sts[...] = dot(sta[...], order, ((0,), (0,))).astype(BF16)

    def sx_copy(q):
        return pltpu.make_async_remote_copy(
            src_ref=sts, dst_ref=inc.at[q], send_sem=sx_sem.at[0, 0], recv_sem=sx_sem.at[1, q],
            device_id=(0, b, m), device_id_type=MESH)

    @pl.when(s == 0)
    def _():
        inc[0] = sts[...]

    @pl.when(s > 0)
    def _():
        sx_copy(s).start()

    lane = iota((BQ, HEADS), 1)
    first = iota((BQ, BQ), 1) < 64
    for k in range(NCH):
        rows = slice(k * BQ, (k + 1) * BQ)

        def pair(j, _, k=k, rows=rows):
            lanes = pl.ds(pl.multiple_of(j * 128, 128), 128)
            cum = cum_v[rows, :]
            sides = []
            for i in range(2):
                h = 2 * j + i
                column = jnp.sum(jnp.where(lane == h, cum, 0.0), axis=1, keepdims=True)
                spread = column - cumt_v[pl.ds(k * HEADS + h, 1), :]
                sides.append((jnp.exp2(jnp.minimum(spread, 0.0)) * g_v[k]).astype(BF16))
            xp = x_v[rows, lanes]
            zero = jnp.zeros_like(xp)
            both = jnp.concatenate([jnp.where(first, xp, zero), jnp.where(first, zero, xp)], axis=0)
            y_v[rows, lanes] = dot(jnp.concatenate(sides, axis=1), both)
            return 0

        lax.fori_loop(0, HEADS // 2, pair, 0)

    right, left = lax.rem(s + 1, SEQ), lax.rem(s + SEQ - 1, SEQ)
    across = lax.rem(s + 2, SEQ)

    def ag_copy(i, part, q, to):
        return pltpu.make_async_remote_copy(
            src_ref=kvall.at[q, part], dst_ref=kvall.at[q, part], send_sem=ag_sem.at[0, i], recv_sem=ag_sem.at[1, i],
            device_id=(to, b, m), device_id_type=MESH)

    for part in range(2):
        each_peer(lambda d, part=part: kv_copy(part, d, False).wait_recv())

        def in_order(e, _, part=part):
            kvall[s, part, pl.ds(pl.multiple_of(e * 16, 16), 16), :] = arrived[part][jnp.clip(pos_s[0, e], 0, OWN * CAP - 1)]
            return 0

        lax.fori_loop(0, ENT, in_order, 0)
        ag_copy(part, part, s, right).start()
        ag_copy(2 + part, part, s, left).start()

    def ch_copy(g):
        return pltpu.make_async_remote_copy(
            src_ref=snd.at[g], dst_ref=inc.at[g], send_sem=ch_sem.at[0, g], recv_sem=ch_sem.at[1, g],
            device_id=(lax.rem(s + 1, SEQ), b, m), device_id_type=MESH)

    for g in range(SEQ):
        lanes = slice(g * KEYS, (g + 1) * KEYS)
        if g > 0:
            @pl.when(s == 0)
            def _(g=g):
                sx_copy(g).wait_recv()

        @pl.when(s > 0)
        def _(g=g):
            ch_copy(g).wait_recv()

        @pl.when(s < SEQ - 1)
        def _(g=g, lanes=lanes):
            snd[g] = (thr_v[3:4, lanes] * inc[g].astype(F32) + lend_v[:, lanes]).astype(BF16)
            ch_copy(g).start()

    loads[5].wait()
    m_v[...] = jnp.full(m_v.shape, NEGATIVE, F32)
    acc_v[...] = jnp.zeros(acc_v.shape, F32)

    def attend(key_ref, value_ref, change):
        def head(h, _):
            at = pl.ds(pl.multiple_of(h * HD, HD), HD)
            shared = pl.ds(pl.multiple_of((h // 4) * HD, HD), HD)
            scores = dot(q_v[:, at], key_ref[:, shared], ((1,), (1,)))
            if change is not None:
                scores = change(scores)
            before = m_v[h]
            now = jnp.maximum(before, jnp.max(scores, axis=1, keepdims=True))
            m_v[h] = now
            width = scores.shape[1] // 128
            probs = jnp.exp2((scores - jnp.concatenate([now] * width, axis=1)) * SCALE2).astype(BF16)
            values = value_ref[:, shared]
            values = jnp.concatenate([values, jnp.ones_like(values)], axis=1)
            shrink = jnp.exp2((before - now) * SCALE2)
            acc_v[h] = acc_v[h] * jnp.concatenate([shrink, shrink], axis=1) + dot(probs, values)
            return 0

        lax.fori_loop(0, QH, head, 0)

    def causal(scores):
        return jnp.where(iota((T, T), 1) <= iota((T, T), 0), scores, NEGATIVE)

    attend(nkv.at[s, 0], nkv.at[s, 1], causal)
    for d in range(1, SEQ):
        @pl.when(s - d >= 0)
        def _(d=d):
            nk_copy(d, False).wait_recv()

    def earlier(j, _):
        attend(nkv.at[j, 0], nkv.at[j, 1], None)
        return 0

    lax.fori_loop(0, s, earlier, 0)
    allowed = iota((1, KEYS), 1) < cached[0] * 16
    bias = jnp.where(allowed, 0.0, NEGATIVE)

    def masked(scores):
        return scores + bias

    attend(kvall.at[s, 0], kvall.at[s, 1], masked)
    for part in range(2):
        ag_copy(part, part, left, right).wait_recv()
    ag_copy(4, 0, left, right).start()
    for part in range(2):
        ag_copy(2 + part, part, right, left).wait_recv()
    ag_copy(5, 1, right, left).start()
    attend(kvall.at[left, 0], kvall.at[left, 1], masked)
    attend(kvall.at[right, 0], kvall.at[right, 1], masked)

    loads[6].wait()

    def gate_tile(j, sums):
        lanes = pl.ds(pl.multiple_of(j * LT, LT), LT)
        state = inc[j // 2, :, pl.ds(pl.multiple_of((j % 2) * LT, LT), LT)].astype(F32)
        out = []
        for k in range(NCH):
            rows = slice(k * BQ, (k + 1) * BQ)
            carried = dot(c_ref[rows, :], state.astype(BF16)) * dot(ecx_v[rows, :], e2_v[:, lanes])
            y = y_v[rows, lanes] + carried + thr_v[4:5, lanes] * x_v[rows, lanes].astype(F32)
            z = z_v[rows, lanes].astype(F32)
            gated = y * (z / (1.0 + jnp.exp(-z)))
            y_v[rows, lanes] = gated
            square = gated * gated
            out.append(sums[k] + square[:, :128] + square[:, 128:])
            if k < NCH - 1:
                state = thr_v[k : k + 1, lanes] * state + l_v[k, :, lanes]
        return tuple(out)

    sums = lax.fori_loop(0, CH // LT, gate_tile, tuple(jnp.zeros((BQ, 128), F32) for _ in range(NCH)))
    ssx[m] = jnp.zeros((8, 128), F32)
    for k in range(NCH):
        ssx[m, k : k + 1, :] = jnp.sum(sums[k].T, axis=0, keepdims=True)

    def mp_copy(d, to):
        other = lax.rem(m + d, MPS) if to else lax.rem(m + MPS - d, MPS)
        at = m if to else other
        return pltpu.make_async_remote_copy(
            src_ref=ssx.at[at], dst_ref=ssx.at[at], send_sem=mp_sem.at[0, d], recv_sem=mp_sem.at[1, d],
            device_id=(s, b, other), device_id_type=MESH)

    for d in range(1, MPS):
        mp_copy(d, True).start()

    ag_copy(4, 0, across, right).wait_recv()
    ag_copy(5, 1, across, left).wait_recv()
    attend(kvall.at[across, 0], kvall.at[across, 1], masked)

    def attn_out(h, _):
        at = pl.ds(pl.multiple_of(h * HD, HD), HD)
        both = acc_v[h]
        attn_ref[:, at] = (both[:, :HD] / both[:, HD:] * valid).astype(BF16)
        return 0

    lax.fori_loop(0, QH, attn_out, 0)

    for d in range(1, MPS):
        mp_copy(d, False).wait_recv()
    whole = ssx[0] + ssx[1] + ssx[2] + ssx[3]
    factor = lax.rsqrt(whole / (HEADS * 64 * MPS) + EPSILON)
    for k in range(NCH):
        rows = slice(k * BQ, (k + 1) * BQ)
        scale = jnp.broadcast_to(factor[k : k + 1], (BQ, BQ)).T * valid[rows]

        def norm_tile(j, _, rows=rows, scale=scale):
            lanes = pl.ds(pl.multiple_of(j * LT, LT), LT)
            ssm_ref[rows, lanes] = (y_v[rows, lanes] * jnp.concatenate([scale, scale], axis=1) * gain_ref[:, lanes]).astype(BF16)
            return 0

        lax.fori_loop(0, CH // LT, norm_tile, 0)

    each_peer(lambda d: tab_copy(d).wait_send())
    each_peer(lambda d: st_copy(d, True).wait_send())
    for part in range(2):
        each_peer(lambda d, part=part: kv_copy(part, d, True).wait_send())
    for d in range(1, SEQ):
        @pl.when(s + d < SEQ)
        def _(d=d):
            nk_copy(d, True).wait_send()

    @pl.when(s > 0)
    def _():
        sx_copy(s).wait_send()

    for part in range(2):
        ag_copy(part, part, s, right).wait_send()
        ag_copy(2 + part, part, s, left).wait_send()
    ag_copy(4, 0, left, right).wait_send()
    ag_copy(5, 1, right, left).wait_send()

    @pl.when(s < SEQ - 1)
    def _():
        for g in range(SEQ):
            ch_copy(g).wait_send()

    for d in range(1, MPS):
        mp_copy(d, True).wait_send()


def per_device(
    xs, gate_z, b_in, c_in, log_decay, d_skip, norm_gain, queries, keys_new, values_new,
    kv_pool, state_pool, new_len, cached_blocks, kv_owner, kv_slot, state_owner, state_slot,
):
    lists = jnp.concatenate([kv_owner[:, :, 0], kv_slot, state_owner[:, :, 0], state_slot], axis=0)
    meta = jnp.pad(lists, ((0, 4), (0, 128 - ENT)))
    pieces = state_pool.reshape(state_pool.shape[0], 2 * HEADS, NS)
    vmem, smem = pl.BlockSpec(memory_space=pltpu.VMEM), pl.BlockSpec(memory_space=pltpu.SMEM)
    hbm = pl.BlockSpec(memory_space=pl.ANY)
    scratch = [
        pltpu.VMEM((T, CH), BF16),
        pltpu.VMEM((T, CH), BF16),
        pltpu.VMEM((T, QH * HD), BF16),
        pltpu.VMEM((SEQ, 2, T, 2 * HD), BF16),
        pltpu.VMEM((32, 2, 16, 2 * HD), BF16),
        pltpu.VMEM((64, 16, NS), BF16),
        pltpu.VMEM((OWN, 1, 128), I32),
        pltpu.VMEM((OWN, 1, 128), I32),
        pltpu.VMEM((8, 128), I32),
        pltpu.SMEM((OWN, 1, 128), I32),
        pltpu.SMEM((8, 128), I32),
        pltpu.VMEM((2, OWN * CAP, 16, 2 * HD), BF16),
        pltpu.VMEM((OWN * CAP, 16, 2 * HD), BF16),
        pltpu.VMEM((OWN * CAP, 16, 2 * HD), BF16),
        pltpu.VMEM((SEQ, 2, KEYS, 2 * HD), BF16),
        pltpu.VMEM((OWN * CAP, 16, NS), BF16),
        pltpu.VMEM((OWN * CAP, 16, NS), BF16),
        pltpu.VMEM((KEYS, NS), BF16),
        pltpu.VMEM((NS, KEYS), BF16),
        pltpu.VMEM((SEQ, NS, KEYS), BF16),
        pltpu.VMEM((SEQ, NS, KEYS), BF16),
        pltpu.VMEM((MPS, 8, 128), F32),
        pltpu.VMEM((T, HEADS), F32),
        pltpu.VMEM((NCH * HEADS, BQ), F32),
        pltpu.VMEM((T, 2 * HEADS), BF16),
        pltpu.VMEM((2 * HEADS, CH), BF16),
        pltpu.VMEM((16, CH), F32),
        pltpu.VMEM((NCH, BQ, BQ), F32),
        pltpu.VMEM((NS, T), BF16),
        pltpu.VMEM((T, 2 * HEADS), BF16),
        pltpu.VMEM((NCH - 1, NS, CH), F32),
        pltpu.VMEM((NS, CH), F32),
        pltpu.VMEM((T, CH), F32),
        pltpu.VMEM((QH, T, 128), F32),
        pltpu.VMEM((QH, T, 2 * HD), F32),
        pltpu.SemaphoreType.DMA((9,)),
        pltpu.SemaphoreType.DMA((2, OWN)),
        pltpu.SemaphoreType.DMA((2, 2, OWN)),
        pltpu.SemaphoreType.DMA((2, OWN)),
        pltpu.SemaphoreType.DMA((2, 6)),
        pltpu.SemaphoreType.DMA((2, SEQ)),
        pltpu.SemaphoreType.DMA((2, SEQ)),
        pltpu.SemaphoreType.DMA((2, SEQ)),
        pltpu.SemaphoreType.DMA((2, MPS)),
    ]
    ssm, attn = pl.pallas_call(
        kernel,
        name="prefill",
        out_shape=(jax.ShapeDtypeStruct((T, CH), BF16), jax.ShapeDtypeStruct((T, QH * HD), BF16)),
        in_specs=[smem, smem] + [vmem] * 6 + [hbm] * 7,
        out_specs=(vmem, vmem),
        scratch_shapes=scratch,
        compiler_params=pltpu.CompilerParams(
            collective_id=0, has_side_effects=True, vmem_limit_bytes=56 * 1024 * 1024),
    )(
        new_len, cached_blocks, meta, b_in[0], c_in[0], log_decay[0], d_skip.reshape(1, HEADS),
        norm_gain.reshape(1, CH), xs[0], gate_z[0], queries[0], keys_new[0], values_new[0], kv_pool, pieces,
    )
    return (ssm[None], attn[None])


def solution(mesh):
    in_specs = (
        P("batch", "seq", "mp"),
        P("batch", "seq", "mp"),
        P("batch", "seq", None),
        P("batch", "seq", None),
        P("batch", "seq", "mp"),
        P("mp"),
        P("mp"),
        P("batch", "seq", "mp"),
        P("batch", "seq", "mp"),
        P("batch", "seq", "mp"),
        P("batch", None, None, "mp"),
        P("batch", "mp", None, None),
        P("batch"),
        P("batch"),
        P("batch", None, None),
        P("batch", None),
        P("batch", None, None),
        P("batch", None),
    )
    out_specs = (P("batch", "seq", "mp"), P("batch", "seq", "mp"))
    return jax.shard_map(
        per_device, mesh=mesh, in_specs=in_specs, out_specs=out_specs, check_vma=False
    )
```

```python
import functools

import jax
import jax.numpy as jnp
from jax import lax
from jax.experimental import pallas as pl
from jax.experimental.pallas import tpu as pltpu
from jax.sharding import PartitionSpec as P

T = 384
CH = 2048
HEADS = 32
NS = 128
BQ = 128
NCH = T // BQ
CAP = 3
OWN = 16
SEQ = 4
MPS = 4
ENT = 32
QH = 8
HD = 128
KEYS = 512
LT = 256
EPSILON = 1e-05
NEGATIVE = -1e30
LOG2E = 1.4426950408889634
SCALE2 = HD ** (-0.5) * LOG2E
MESH = pl.DeviceIdType.MESH
F32, BF16, I32 = jnp.float32, jnp.bfloat16, jnp.int32


def iota(shape, dim):
    return lax.broadcasted_iota(I32, shape, dim)


def dot(a, b, dims=((1,), (0,)), precision=None):
    return lax.dot_general(
        a, b, (dims, ((), ())), precision=precision, preferred_element_type=F32
    )


def high_low(v):
    high = v.astype(BF16)
    return jnp.concatenate([high, (v - high.astype(F32)).astype(BF16)], axis=1)


def ranks_of(owner):
    lane, row = iota((ENT, ENT), 1), iota((ENT, ENT), 0)
    column = jnp.sum(jnp.where(lane == row, owner, 0), axis=1, keepdims=True)
    same = (column == owner) & (row < lane)
    return jnp.sum(jnp.where(same, 1, 0), axis=0, keepdims=True)


def kernel(
    new_len, cached, ko_ref, kl_ref, so_ref, sl_ref, b_ref, c_ref, ld_ref, dsk_ref, gain_ref,
    x_hbm, z_hbm, q_hbm, k_hbm, v_hbm, kvp_hbm, stp_hbm,
    ssm_ref, attn_ref,
    x_v, z_v, q_v, nkv, kvq, stq, tab_v, rtab_v, pos_v, rtab_s, pos_s,
    skv, rk, rv, kvall, sst, rst, sta, sts, inc, snd, ssx,
    cum_v, cumt_v, ecx_v, e2_v, thr_v, g_v, bt_v, rem_v, l_v, lend_v, y_v, qs_v, weigh_v, m_v, acc_v,
    load_sem, tab_sem, z_sem, st_sem, ag_sem, nk_sem, sx_sem, ch_sem, mp_sem,
):
    arrived = (rk, rv)
    s, b, m = lax.axis_index("seq"), lax.axis_index("batch"), lax.axis_index("mp")

    quarter = pl.ds(pl.multiple_of(s * 16, 16), 16)
    loads = [
        pltpu.make_async_copy(stp_hbm.at[:, quarter, :], stq, load_sem.at[0]),
        pltpu.make_async_copy(kvp_hbm.at[:, :, quarter, :], kvq, load_sem.at[1]),
        pltpu.make_async_copy(k_hbm, nkv.at[s, 0], load_sem.at[2]),
        pltpu.make_async_copy(v_hbm, nkv.at[s, 1], load_sem.at[3]),
        pltpu.make_async_copy(x_hbm, x_v, load_sem.at[4]),
        pltpu.make_async_copy(q_hbm, q_v, load_sem.at[5]),
        pltpu.make_async_copy(z_hbm, z_v, load_sem.at[6]),
    ]
    for load in loads:
        load.start()

    barrier = pltpu.get_barrier_semaphore()

    def greet(d, _):
        pl.semaphore_signal(barrier, inc=1, device_id=(s, lax.rem(b + d, OWN), m), device_id_type=MESH)
        return 0

    lax.fori_loop(1, OWN, greet, 0)
    for d in range(1, SEQ):
        pl.semaphore_signal(barrier, inc=1, device_id=(lax.rem(s + d, SEQ), b, m), device_id_type=MESH)
    for d in range(1, MPS):
        pl.semaphore_signal(barrier, inc=1, device_id=(s, b, lax.rem(m + d, MPS)), device_id_type=MESH)

    lane16, row16 = iota((OWN, 128), 1), iota((OWN, ENT), 0)
    table = jnp.zeros((OWN, 128), I32)
    for part, (owner_ref, slot_ref) in enumerate(((ko_ref, kl_ref), (so_ref, sl_ref))):
        owner, slot = owner_ref[...], slot_ref[...]
        rank = ranks_of(owner)
        pos_v[part : part + 1, :ENT] = jnp.clip(owner * CAP + rank, 0, OWN * CAP - 1)
        for c in range(CAP):
            hit = (owner == row16) & (rank == c)
            asked = jnp.sum(jnp.where(hit, slot, 0), axis=1, keepdims=True)
            table = jnp.where(lane16 == part * CAP + c, asked, table)
    for o in range(OWN):
        tab_v[o] = table[o : o + 1]
    rtab_v[b] = tab_v[b]
    to_pos = pltpu.make_async_copy(pos_v, pos_s, load_sem.at[7])
    to_pos.start()

    pl.semaphore_wait(barrier, OWN - 1 + SEQ - 1 + MPS - 1)

    def tab_copy(d):
        peer = lax.rem(b + d, OWN)
        return pltpu.make_async_remote_copy(
            src_ref=tab_v.at[peer], dst_ref=rtab_v.at[b], send_sem=tab_sem.at[0, d], recv_sem=tab_sem.at[1, d],
            device_id=(s, peer, m), device_id_type=MESH)

    def tab_from(d):
        source = lax.rem(b + OWN - d, OWN)
        return pltpu.make_async_remote_copy(
            src_ref=tab_v.at[source], dst_ref=rtab_v.at[source], send_sem=tab_sem.at[0, d], recv_sem=tab_sem.at[1, d],
            device_id=(s, source, m), device_id_type=MESH)

    def st_copy(d, to):
        peer = lax.rem(b + d, OWN) if to else lax.rem(b + OWN - d, OWN)
        at = b if to else peer
        return pltpu.make_async_remote_copy(
            src_ref=sst.at[pl.ds(peer * CAP, CAP)], dst_ref=rst.at[pl.ds(at * CAP, CAP)],
            send_sem=st_sem.at[0, d], recv_sem=st_sem.at[1, d], device_id=(s, peer, m), device_id_type=MESH)

    def kv_copy(part, d, to):
        peer = lax.rem(b + d, OWN) if to else lax.rem(b + OWN - d, OWN)
        at = b if to else peer
        return pltpu.make_async_remote_copy(
            src_ref=skv.at[part, pl.ds(peer * CAP, CAP)], dst_ref=arrived[part].at[pl.ds(at * CAP, CAP)],
            send_sem=z_sem.at[0, part, d], recv_sem=z_sem.at[1, part, d], device_id=(s, peer, m), device_id_type=MESH)

    def each_peer(act):
        def one(d, _):
            act(d)
            return 0

        lax.fori_loop(1, OWN, one, 0)

    each_peer(lambda d: tab_copy(d).start())

    loads[2].wait()
    loads[3].wait()

    right, left = lax.rem(s + 1, SEQ), lax.rem(s + SEQ - 1, SEQ)
    across = lax.rem(s + 2, SEQ)

    def nk_copy(slot, way):
        return pltpu.make_async_remote_copy(
            src_ref=nkv.at[slot], dst_ref=nkv.at[slot], send_sem=nk_sem.at[0, slot, way], recv_sem=nk_sem.at[1, slot, way],
            device_id=(left if way else right, b, m), device_id_type=MESH)

    hops = ((0, 0, 0), (1, 1, 0), (2, 2, 0), (1, 1, 1), (0, 0, 1))
    onward = ((0, 1, 1), (3, 0, 1))

    def nk_send(who, slot, way):
        @pl.when(s == who)
        def _():
            nk_copy(slot, way).start()

    def nk_arrive(who, slot, way):
        @pl.when(s == (who + SEQ - 1 if way else who + 1) % SEQ)
        def _():
            nk_copy(slot, way).wait_recv()

    for hop in hops:
        nk_send(*hop)

    tri = jnp.where(iota((BQ, BQ), 0) >= iota((BQ, BQ), 1), 1.0, 0.0)
    triu = jnp.where(iota((BQ, BQ), 0) <= iota((BQ, BQ), 1), 1.0, 0.0)
    valid = jnp.where(s * T + iota((T, 1), 0) < new_len[0], 1.0, 0.0)
    valid_row = jnp.where(s * T + iota((1, T), 1) < new_len[0], 1.0, 0.0)
    e2_v[...] = jnp.where((iota((2 * HEADS, CH), 0) & (HEADS - 1)) == (iota((2 * HEADS, CH), 1) >> 6), 1.0, 0.0).astype(BF16)
    totals = []
    for k in range(NCH):
        rows = slice(k * BQ, (k + 1) * BQ)
        dec = ld_ref[:, rows] * valid_row[:, rows]
        cum = dot(tri, dec, ((1,), (1,)), lax.Precision.HIGHEST)
        cumt_v[k * HEADS : (k + 1) * HEADS, :] = LOG2E * dot(dec, triu, precision=lax.Precision.HIGHEST)
        cum_v[rows, :] = LOG2E * cum
        total = cum[BQ - 1 : BQ]
        totals.append(total)
        ecx_v[rows, :] = high_low(jnp.exp(cum))
        rem_v[rows, :] = high_low(jnp.exp(total - cum) * valid[rows])
        bt_v[:, rows] = b_ref[rows, :].astype(F32).T.astype(BF16)
        g = dot(c_ref[rows, :], b_ref[rows, :], ((1,), (1,)))
        g_v[k] = g * tri
    row = iota((16, HEADS), 0)
    small = jnp.where(row == 3, jnp.exp(totals[0] + totals[1] + totals[2]), jnp.where(row == 4, dsk_ref[...], 0.0))
    for k in range(NCH):
        small = jnp.where(row == k, jnp.exp(totals[k]), small)
    thr_v[...] = dot(high_low(small), e2_v[...])

    each_peer(lambda d: tab_from(d).wait_recv())
    to_tab = pltpu.make_async_copy(rtab_v, rtab_s, load_sem.at[8])
    to_tab.start()
    to_tab.wait()
    to_pos.wait()
    loads[0].wait()

    def pack_state(i, _):
        for c in range(CAP):
            sst[i * CAP + c] = stq[jnp.clip(rtab_s[i, 0, CAP + c], 0, 63)]
        return 0

    lax.fori_loop(0, OWN, pack_state, 0)
    each_peer(lambda d: st_copy(d, True).start())
    loads[1].wait()
    for part in range(2):
        def pack_kv(i, _, part=part):
            for c in range(CAP):
                skv[part, i * CAP + c] = kvq[jnp.clip(rtab_s[i, 0, c], 0, 31), part]
            return 0

        lax.fori_loop(0, OWN, pack_kv, 0)
        each_peer(lambda d, part=part: kv_copy(part, d, True).start())
    for c in range(CAP):
        rst[b * CAP + c] = sst[b * CAP + c]
        for part in range(2):
            arrived[part][b * CAP + c] = skv[part, b * CAP + c]

    loads[4].wait()

    def end_tile(j, _):
        lanes = pl.ds(pl.multiple_of(j * LT, LT), LT)
        total = None
        for k in range(NCH):
            rows = slice(k * BQ, (k + 1) * BQ)
            xr = (x_v[rows, lanes].astype(F32) * dot(rem_v[rows, :], e2_v[:, lanes])).astype(BF16)
            part = dot(bt_v[:, rows], xr)
            if k < NCH - 1:
                l_v[k, :, lanes] = part
            total = part if k == 0 else thr_v[k : k + 1, lanes] * total + part
        lend_v[:, lanes] = total
        return 0

    lax.fori_loop(0, CH // LT, end_tile, 0)

    each_peer(lambda d: st_copy(d, False).wait_recv())

    def place(j, _):
        sta[pl.ds(pl.multiple_of(j * 16, 16), 16), :] = rst[jnp.clip(pos_s[1, j], 0, OWN * CAP - 1)]
        return 0

    lax.fori_loop(0, ENT, place, 0)
    r, c = iota((KEYS, KEYS), 0), iota((KEYS, KEYS), 1)
    order = jnp.where(c == ((r >> 1) & 7) * 64 + (r >> 4) * 2 + (r & 1), 1.0, 0.0).astype(BF16)
    sts[...] = dot(sta[...], order, ((0,), (0,))).astype(BF16)

    def sx_copy(q):
        return pltpu.make_async_remote_copy(
            src_ref=sts, dst_ref=inc.at[q], send_sem=sx_sem.at[0, 0], recv_sem=sx_sem.at[1, q],
            device_id=(0, b, m), device_id_type=MESH)

    @pl.when(s == 0)
    def _():
        inc[0] = sts[...]

    @pl.when(s > 0)
    def _():
        sx_copy(s).start()

    first = iota((BQ, BQ), 1) < 64

    def within(k, _):
        rows = pl.ds(pl.multiple_of(k * BQ, BQ), BQ)
        cum = cum_v[rows, :]
        cumt = cumt_v[pl.ds(pl.multiple_of(k * HEADS, HEADS), HEADS), :]
        g = g_v[k]
        for j in range(HEADS // 2):
            lanes = slice(j * 128, (j + 1) * 128)
            sides = []
            for h in (2 * j, 2 * j + 1):
                spread = cum[:, h : h + 1] - cumt[h : h + 1, :]
                sides.append((jnp.exp2(jnp.minimum(spread, 0.0)) * g).astype(BF16))
            xp = x_v[rows, lanes]
            zero = jnp.zeros_like(xp)
            both = jnp.concatenate([jnp.where(first, xp, zero), jnp.where(first, zero, xp)], axis=0)
            y_v[rows, lanes] = dot(jnp.concatenate(sides, axis=1), both)
        return 0

    lax.fori_loop(0, NCH, within, 0)

    def ag_copy(i, part, q, to):
        return pltpu.make_async_remote_copy(
            src_ref=kvall.at[q, part], dst_ref=kvall.at[q, part], send_sem=ag_sem.at[0, i], recv_sem=ag_sem.at[1, i],
            device_id=(to, b, m), device_id_type=MESH)

    def put_in_order(part):
        each_peer(lambda d: kv_copy(part, d, False).wait_recv())
        nothing = jnp.zeros((16, 2 * HD), BF16)

        def in_order(e, _):
            to = pl.ds(pl.multiple_of(e * 16, 16), 16)
            listed = e < cached[0]
            place_of = pos_s[0, e] if part else jnp.where(listed, pos_s[0, e], pos_s[0, 0])
            rows = arrived[part][jnp.clip(place_of, 0, OWN * CAP - 1)]
            kvall[s, part, to, :] = jnp.where(listed, rows, nothing) if part else rows
            return 0

        lax.fori_loop(0, ENT, in_order, 0)
        ag_copy(part, part, s, right).start()
        ag_copy(2 + part, part, s, left).start()

    def ch_copy(g):
        return pltpu.make_async_remote_copy(
            src_ref=snd.at[g], dst_ref=inc.at[g], send_sem=ch_sem.at[0, g], recv_sem=ch_sem.at[1, g],
            device_id=(lax.rem(s + 1, SEQ), b, m), device_id_type=MESH)

    def chain(who):
        @pl.when(s == who)
        def _():
            for g in range(SEQ):
                lanes = slice(g * KEYS, (g + 1) * KEYS)
                if who == 0 and g > 0:
                    sx_copy(g).wait_recv()
                if who > 0:
                    ch_copy(g).wait_recv()
                if who < SEQ - 1:
                    snd[g] = (thr_v[3:4, lanes] * inc[g].astype(F32) + lend_v[:, lanes]).astype(BF16)
                    ch_copy(g).start()

    loads[5].wait()
    for h in range(QH):
        qs_v[h] = high_low(q_v[:, h * HD : (h + 1) * HD].astype(F32) * SCALE2)
    m_v[...] = jnp.full(m_v.shape, NEGATIVE, F32)
    acc_v[...] = jnp.zeros(acc_v.shape, F32)

    def attend(key_ref, value_ref, change, weigh):
        def group(g, _):
            shared = pl.ds(pl.multiple_of(g * HD, HD), HD)
            keys = key_ref[:, shared]
            keys = jnp.concatenate([keys, keys], axis=1)
            values = value_ref[:, shared]
            values = jnp.concatenate([values, jnp.ones_like(values) if weigh is None else weigh[...]], axis=1)
            for i in range(4):
                scores = dot(qs_v[4 * g + i], keys, ((1,), (1,)))
                if change is not None:
                    scores = change(scores)
                before = m_v[g, i]
                now = jnp.maximum(before, jnp.max(scores, axis=1, keepdims=True))
                m_v[g, i] = now
                width = scores.shape[1] // 128
                probs = jnp.exp2(scores - jnp.concatenate([now] * width, axis=1)).astype(BF16)
                shrink = jnp.exp2(before - now)
                acc_v[g, i] = acc_v[g, i] * jnp.concatenate([shrink, shrink], axis=1) + dot(probs, values)
            return 0

        lax.fori_loop(0, QH // 4, group, 0, unroll=2)

    def causal(scores):
        return jnp.where(iota((T, T), 1) <= iota((T, T), 0), scores, NEGATIVE)

    nk_arrive(1, 1, 1)
    nk_arrive(0, 0, 1)
    for hop in onward:
        nk_send(*hop)
    chain(0)
    put_in_order(0)
    attend(nkv.at[s, 0], nkv.at[s, 1], causal, None)
    chain(1)
    put_in_order(1)
    chain(2)
    for hop in (hops[:3] + onward):
        nk_arrive(*hop)

    def earlier(j, _):
        attend(nkv.at[j, 0], nkv.at[j, 1], None, None)
        return 0

    lax.fori_loop(0, s, earlier, 0)
    weigh_v[...] = jnp.where(iota((KEYS, HD), 0) < cached[0] * 16, 1.0, 0.0).astype(BF16)
    attend(kvall.at[s, 0], kvall.at[s, 1], None, weigh_v)
    ag_copy(0, 0, left, right).wait_recv()
    ag_copy(4, 0, left, right).start()
    ag_copy(2, 0, right, left).wait_recv()
    ag_copy(3, 1, right, left).wait_recv()
    ag_copy(5, 1, right, left).start()
    ag_copy(1, 1, left, right).wait_recv()
    attend(kvall.at[left, 0], kvall.at[left, 1], None, weigh_v)
    attend(kvall.at[right, 0], kvall.at[right, 1], None, weigh_v)
    chain(3)

    loads[6].wait()

    def gate_tile(j, sums):
        lanes = pl.ds(pl.multiple_of(j * LT, LT), LT)
        state = inc[j // 2, :, pl.ds(pl.multiple_of((j % 2) * LT, LT), LT)].astype(F32)
        out = []
        for k in range(NCH):
            rows = slice(k * BQ, (k + 1) * BQ)
            carried = dot(c_ref[rows, :], state.astype(BF16)) * dot(ecx_v[rows, :], e2_v[:, lanes])
            y = y_v[rows, lanes] + carried + thr_v[4:5, lanes] * x_v[rows, lanes].astype(F32)
            z = z_v[rows, lanes].astype(F32)
            gated = y * (z / (1.0 + jnp.exp(-z)))
            y_v[rows, lanes] = gated
            square = gated * gated
            out.append(sums[k] + square[:, :128] + square[:, 128:])
            if k < NCH - 1:
                state = thr_v[k : k + 1, lanes] * state + l_v[k, :, lanes]
        return tuple(out)

    sums = lax.fori_loop(0, CH // LT, gate_tile, tuple(jnp.zeros((BQ, 128), F32) for _ in range(NCH)))
    ssx[m] = jnp.zeros((8, 128), F32)
    for k in range(NCH):
        ssx[m, k : k + 1, :] = jnp.sum(sums[k].T, axis=0, keepdims=True)

    def mp_copy(d, to):
        other = lax.rem(m + d, MPS) if to else lax.rem(m + MPS - d, MPS)
        at = m if to else other
        return pltpu.make_async_remote_copy(
            src_ref=ssx.at[at], dst_ref=ssx.at[at], send_sem=mp_sem.at[0, d], recv_sem=mp_sem.at[1, d],
            device_id=(s, b, other), device_id_type=MESH)

    for d in range(1, MPS):
        mp_copy(d, True).start()

    ag_copy(4, 0, across, right).wait_recv()
    ag_copy(5, 1, across, left).wait_recv()
    attend(kvall.at[across, 0], kvall.at[across, 1], None, weigh_v)

    def attn_out(h, _):
        at = pl.ds(pl.multiple_of(h * HD, HD), HD)
        both = acc_v[h // 4, h % 4]
        attn_ref[:, at] = (both[:, :HD] / both[:, HD:] * valid).astype(BF16)
        return 0

    lax.fori_loop(0, QH, attn_out, 0)

    for d in range(1, MPS):
        mp_copy(d, False).wait_recv()
    whole = ssx[0] + ssx[1] + ssx[2] + ssx[3]
    factor = lax.rsqrt(whole / (HEADS * 64 * MPS) + EPSILON)
    for k in range(NCH):
        rows = slice(k * BQ, (k + 1) * BQ)
        scale = jnp.broadcast_to(factor[k : k + 1], (BQ, BQ)).T * valid[rows]

        def norm_tile(j, _, rows=rows, scale=scale):
            lanes = pl.ds(pl.multiple_of(j * LT, LT), LT)
            ssm_ref[rows, lanes] = (y_v[rows, lanes] * jnp.concatenate([scale, scale], axis=1) * gain_ref[:, lanes]).astype(BF16)
            return 0

        lax.fori_loop(0, CH // LT, norm_tile, 0)

    each_peer(lambda d: tab_copy(d).wait_send())
    each_peer(lambda d: st_copy(d, True).wait_send())
    for part in range(2):
        each_peer(lambda d, part=part: kv_copy(part, d, True).wait_send())
    for who, slot, way in hops + onward:
        @pl.when(s == who)
        def _(slot=slot, way=way):
            nk_copy(slot, way).wait_send()

    @pl.when(s > 0)
    def _():
        sx_copy(s).wait_send()

    for part in range(2):
        ag_copy(part, part, s, right).wait_send()
        ag_copy(2 + part, part, s, left).wait_send()
    ag_copy(4, 0, left, right).wait_send()
    ag_copy(5, 1, right, left).wait_send()

    @pl.when(s < SEQ - 1)
    def _():
        for g in range(SEQ):
            ch_copy(g).wait_send()

    for d in range(1, MPS):
        mp_copy(d, True).wait_send()


def per_device(
    xs, gate_z, b_in, c_in, log_decay, d_skip, norm_gain, queries, keys_new, values_new,
    kv_pool, state_pool, new_len, cached_blocks, kv_owner, kv_slot, state_owner, state_slot,
):
    pieces = state_pool.reshape(state_pool.shape[0], 2 * HEADS, NS)
    vmem, smem = pl.BlockSpec(memory_space=pltpu.VMEM), pl.BlockSpec(memory_space=pltpu.SMEM)
    hbm = pl.BlockSpec(memory_space=pltpu.HBM)
    scratch = [
        pltpu.VMEM((T, CH), BF16),
        pltpu.VMEM((T, CH), BF16),
        pltpu.VMEM((T, QH * HD), BF16),
        pltpu.VMEM((SEQ, 2, T, 2 * HD), BF16),
        pltpu.VMEM((32, 2, 16, 2 * HD), BF16),
        pltpu.VMEM((64, 16, NS), BF16),
        pltpu.VMEM((OWN, 1, 128), I32),
        pltpu.VMEM((OWN, 1, 128), I32),
        pltpu.VMEM((8, 128), I32),
        pltpu.SMEM((OWN, 1, 128), I32),
        pltpu.SMEM((8, 128), I32),
        pltpu.VMEM((2, OWN * CAP, 16, 2 * HD), BF16),
        pltpu.VMEM((OWN * CAP, 16, 2 * HD), BF16),
        pltpu.VMEM((OWN * CAP, 16, 2 * HD), BF16),
        pltpu.VMEM((SEQ, 2, KEYS, 2 * HD), BF16),
        pltpu.VMEM((OWN * CAP, 16, NS), BF16),
        pltpu.VMEM((OWN * CAP, 16, NS), BF16),
        pltpu.VMEM((KEYS, NS), BF16),
        pltpu.VMEM((NS, KEYS), BF16),
        pltpu.VMEM((SEQ, NS, KEYS), BF16),
        pltpu.VMEM((SEQ, NS, KEYS), BF16),
        pltpu.VMEM((MPS, 8, 128), F32),
        pltpu.VMEM((T, HEADS), F32),
        pltpu.VMEM((NCH * HEADS, BQ), F32),
        pltpu.VMEM((T, 2 * HEADS), BF16),
        pltpu.VMEM((2 * HEADS, CH), BF16),
        pltpu.VMEM((16, CH), F32),
        pltpu.VMEM((NCH, BQ, BQ), F32),
        pltpu.VMEM((NS, T), BF16),
        pltpu.VMEM((T, 2 * HEADS), BF16),
        pltpu.VMEM((NCH - 1, NS, CH), F32),
        pltpu.VMEM((NS, CH), F32),
        pltpu.VMEM((T, CH), F32),
        pltpu.VMEM((QH, T, 2 * HD), BF16),
        pltpu.VMEM((KEYS, HD), BF16),
        pltpu.VMEM((2, QH // 2, T, 128), F32),
        pltpu.VMEM((2, QH // 2, T, 2 * HD), F32),
        pltpu.SemaphoreType.DMA((9,)),
        pltpu.SemaphoreType.DMA((2, OWN)),
        pltpu.SemaphoreType.DMA((2, 2, OWN)),
        pltpu.SemaphoreType.DMA((2, OWN)),
        pltpu.SemaphoreType.DMA((2, 6)),
        pltpu.SemaphoreType.DMA((2, SEQ, 2)),
        pltpu.SemaphoreType.DMA((2, SEQ)),
        pltpu.SemaphoreType.DMA((2, SEQ)),
        pltpu.SemaphoreType.DMA((2, MPS)),
    ]
    ssm, attn = pl.pallas_call(
        kernel,
        name="prefill",
        out_shape=(jax.ShapeDtypeStruct((T, CH), BF16), jax.ShapeDtypeStruct((T, QH * HD), BF16)),
        in_specs=[smem, smem] + [vmem] * 9 + [hbm] * 7,
        out_specs=(vmem, vmem),
        scratch_shapes=scratch,
        compiler_params=pltpu.CompilerParams(
            collective_id=0, has_side_effects=True, vmem_limit_bytes=40 * 1024 * 1024),
    )(
        new_len, cached_blocks, kv_owner[:, :, 0], kv_slot, state_owner[:, :, 0], state_slot,
        b_in[0], c_in[0], log_decay[0].T, d_skip.reshape(1, HEADS),
        norm_gain.reshape(1, CH), xs[0], gate_z[0], queries[0], keys_new[0], values_new[0], kv_pool, pieces,
    )
    return (ssm[None], attn[None])


def solution(mesh):
    in_specs = (
        P("batch", "seq", "mp"),
        P("batch", "seq", "mp"),
        P("batch", "seq", None),
        P("batch", "seq", None),
        P("batch", "seq", "mp"),
        P("mp"),
        P("mp"),
        P("batch", "seq", "mp"),
        P("batch", "seq", "mp"),
        P("batch", "seq", "mp"),
        P("batch", None, None, "mp"),
        P("batch", "mp", None, None),
        P("batch"),
        P("batch"),
        P("batch", None, None),
        P("batch", None),
        P("batch", None, None),
        P("batch", None),
    )
    out_specs = (P("batch", "seq", "mp"), P("batch", "seq", "mp"))
    return jax.shard_map(
        per_device, mesh=mesh, in_specs=in_specs, out_specs=out_specs, check_vma=False
    )
```

```python
import functools

import jax
import jax.numpy as jnp
from jax import lax
from jax.experimental import pallas as pl
from jax.experimental.pallas import tpu as pltpu
from jax.sharding import PartitionSpec as P

T = 384
CH = 2048
HEADS = 32
NS = 128
BQ = 128
NCH = T // BQ
CAP = 3
OWN = 16
SEQ = 4
MPS = 4
ENT = 32
QH = 8
HD = 128
KEYS = 512
LT = 256
EPSILON = 1e-05
NEGATIVE = -1e30
LOG2E = 1.4426950408889634
SCALE2 = HD ** (-0.5) * LOG2E
MESH = pl.DeviceIdType.MESH
F32, BF16, I32 = jnp.float32, jnp.bfloat16, jnp.int32


def iota(shape, dim):
    return lax.broadcasted_iota(I32, shape, dim)


def dot(a, b, dims=((1,), (0,)), precision=None):
    return lax.dot_general(
        a, b, (dims, ((), ())), precision=precision, preferred_element_type=F32
    )


def high_low(v):
    high = v.astype(BF16)
    return jnp.concatenate([high, (v - high.astype(F32)).astype(BF16)], axis=1)


def ranks_of(owner):
    lane, row = iota((ENT, ENT), 1), iota((ENT, ENT), 0)
    column = jnp.sum(jnp.where(lane == row, owner, 0), axis=1, keepdims=True)
    same = (column == owner) & (row < lane)
    return jnp.sum(jnp.where(same, 1, 0), axis=0, keepdims=True)


def kernel(
    new_len, cached, ko_ref, kl_ref, so_ref, sl_ref, b_ref, c_ref, ld_ref, dsk_ref, gain_ref,
    x_hbm, z_hbm, q_hbm, k_hbm, v_hbm, kvp_hbm, stp_hbm,
    ssm_ref, attn_ref,
    x_v, z_v, q_v, nkv, kvq, stq, tab_v, rtab_v, pos_v, rtab_s, pos_s,
    skv, rk, rv, kvall, sst, rst, sta, sts, inc, snd, ssx,
    cum_v, cumt_v, ecx_v, e2_v, thr_v, g_v, bt_v, rem_v, l_v, lend_v, y_v, qs_v, weigh_v, m_v, acc_v,
    load_sem, tab_sem, z_sem, st_sem, ag_sem, nk_sem, sx_sem, ch_sem, mp_sem,
):
    arrived = (rk, rv)
    s, b, m = lax.axis_index("seq"), lax.axis_index("batch"), lax.axis_index("mp")

    quarter = pl.ds(pl.multiple_of(s * 16, 16), 16)
    loads = [
        pltpu.make_async_copy(stp_hbm.at[:, quarter, :], stq, load_sem.at[0]),
        pltpu.make_async_copy(kvp_hbm.at[:, :, quarter, :], kvq, load_sem.at[1]),
        pltpu.make_async_copy(k_hbm, nkv.at[s, 0], load_sem.at[2]),
        pltpu.make_async_copy(v_hbm, nkv.at[s, 1], load_sem.at[3]),
        pltpu.make_async_copy(x_hbm, x_v, load_sem.at[4]),
        pltpu.make_async_copy(q_hbm, q_v, load_sem.at[5]),
        pltpu.make_async_copy(z_hbm, z_v, load_sem.at[6]),
    ]
    for load in loads:
        load.start()

    barrier = pltpu.get_barrier_semaphore()

    def greet(d, _):
        pl.semaphore_signal(barrier, inc=1, device_id=(s, lax.rem(b + d, OWN), m), device_id_type=MESH)
        return 0

    lax.fori_loop(1, OWN, greet, 0)
    for d in range(1, SEQ):
        pl.semaphore_signal(barrier, inc=1, device_id=(lax.rem(s + d, SEQ), b, m), device_id_type=MESH)
    for d in range(1, MPS):
        pl.semaphore_signal(barrier, inc=1, device_id=(s, b, lax.rem(m + d, MPS)), device_id_type=MESH)

    lane16, row16 = iota((OWN, 128), 1), iota((OWN, ENT), 0)
    table = jnp.zeros((OWN, 128), I32)
    for part, (owner_ref, slot_ref) in enumerate(((ko_ref, kl_ref), (so_ref, sl_ref))):
        owner, slot = owner_ref[...], slot_ref[...]
        rank = ranks_of(owner)
        pos_v[part : part + 1, :ENT] = jnp.clip(owner * CAP + rank, 0, OWN * CAP - 1)
        for c in range(CAP):
            hit = (owner == row16) & (rank == c)
            asked = jnp.sum(jnp.where(hit, slot, 0), axis=1, keepdims=True)
            table = jnp.where(lane16 == part * CAP + c, asked, table)
    for o in range(OWN):
        tab_v[o] = table[o : o + 1]
    rtab_v[b] = tab_v[b]
    to_pos = pltpu.make_async_copy(pos_v, pos_s, load_sem.at[7])
    to_pos.start()

    pl.semaphore_wait(barrier, OWN - 1 + SEQ - 1 + MPS - 1)

    def tab_copy(d):
        peer = lax.rem(b + d, OWN)
        return pltpu.make_async_remote_copy(
            src_ref=tab_v.at[peer], dst_ref=rtab_v.at[b], send_sem=tab_sem.at[0, d], recv_sem=tab_sem.at[1, d],
            device_id=(s, peer, m), device_id_type=MESH)

    def tab_from(d):
        source = lax.rem(b + OWN - d, OWN)
        return pltpu.make_async_remote_copy(
            src_ref=tab_v.at[source], dst_ref=rtab_v.at[source], send_sem=tab_sem.at[0, d], recv_sem=tab_sem.at[1, d],
            device_id=(s, source, m), device_id_type=MESH)

    def st_copy(d, to):
        peer = lax.rem(b + d, OWN) if to else lax.rem(b + OWN - d, OWN)
        at = b if to else peer
        return pltpu.make_async_remote_copy(
            src_ref=sst.at[pl.ds(peer * CAP, CAP)], dst_ref=rst.at[pl.ds(at * CAP, CAP)],
            send_sem=st_sem.at[0, d], recv_sem=st_sem.at[1, d], device_id=(s, peer, m), device_id_type=MESH)

    def kv_copy(part, d, to):
        peer = lax.rem(b + d, OWN) if to else lax.rem(b + OWN - d, OWN)
        at = b if to else peer
        return pltpu.make_async_remote_copy(
            src_ref=skv.at[part, pl.ds(peer * CAP, CAP)], dst_ref=arrived[part].at[pl.ds(at * CAP, CAP)],
            send_sem=z_sem.at[0, part, d], recv_sem=z_sem.at[1, part, d], device_id=(s, peer, m), device_id_type=MESH)

    def each_peer(act):
        def one(d, _):
            act(d)
            return 0

        lax.fori_loop(1, OWN, one, 0)

    each_peer(lambda d: tab_copy(d).start())

    loads[2].wait()
    loads[3].wait()

    right, left = lax.rem(s + 1, SEQ), lax.rem(s + SEQ - 1, SEQ)
    across = lax.rem(s + 2, SEQ)

    def nk_copy(slot, way):
        return pltpu.make_async_remote_copy(
            src_ref=nkv.at[slot], dst_ref=nkv.at[slot], send_sem=nk_sem.at[0, slot, way], recv_sem=nk_sem.at[1, slot, way],
            device_id=(left if way else right, b, m), device_id_type=MESH)

    hops = ((0, 0, 0), (1, 1, 0), (2, 2, 0), (1, 1, 1), (0, 0, 1))
    onward = ((0, 1, 1), (3, 0, 1))

    def nk_send(who, slot, way):
        @pl.when(s == who)
        def _():
            nk_copy(slot, way).start()

    def nk_arrive(who, slot, way):
        @pl.when(s == (who + SEQ - 1 if way else who + 1) % SEQ)
        def _():
            nk_copy(slot, way).wait_recv()

    for hop in hops:
        nk_send(*hop)

    tri = jnp.where(iota((BQ, BQ), 0) >= iota((BQ, BQ), 1), 1.0, 0.0)
    triu = jnp.where(iota((BQ, BQ), 0) <= iota((BQ, BQ), 1), 1.0, 0.0)
    valid = jnp.where(s * T + iota((T, 1), 0) < new_len[0], 1.0, 0.0)
    valid_row = jnp.where(s * T + iota((1, T), 1) < new_len[0], 1.0, 0.0)
    e2_v[...] = jnp.where((iota((2 * HEADS, CH), 0) & (HEADS - 1)) == (iota((2 * HEADS, CH), 1) >> 6), 1.0, 0.0).astype(BF16)
    totals = []
    for k in range(NCH):
        rows = slice(k * BQ, (k + 1) * BQ)
        dec = ld_ref[:, rows] * valid_row[:, rows]
        cum = dot(tri, dec, ((1,), (1,)), lax.Precision.HIGHEST)
        cumt_v[k * HEADS : (k + 1) * HEADS, :] = LOG2E * dot(dec, triu, precision=lax.Precision.HIGHEST)
        cum_v[rows, :] = LOG2E * cum
        total = cum[BQ - 1 : BQ]
        totals.append(total)
        ecx_v[rows, :] = high_low(jnp.exp(cum))
        rem_v[rows, :] = high_low(jnp.exp(total - cum) * valid[rows])
        bt_v[:, rows] = b_ref[rows, :].astype(F32).T.astype(BF16)
        g = dot(c_ref[rows, :], b_ref[rows, :], ((1,), (1,)))
        g_v[k] = g * tri
    row = iota((16, HEADS), 0)
    small = jnp.where(row == 3, jnp.exp(totals[0] + totals[1] + totals[2]), jnp.where(row == 4, dsk_ref[...], 0.0))
    for k in range(NCH):
        small = jnp.where(row == k, jnp.exp(totals[k]), small)
    thr_v[...] = dot(high_low(small), e2_v[...])

    each_peer(lambda d: tab_from(d).wait_recv())
    to_tab = pltpu.make_async_copy(rtab_v, rtab_s, load_sem.at[8])
    to_tab.start()
    to_tab.wait()
    to_pos.wait()
    loads[0].wait()

    def pack_state(i, _):
        for c in range(CAP):
            sst[i * CAP + c] = stq[jnp.clip(rtab_s[i, 0, CAP + c], 0, 63)]
        return 0

    lax.fori_loop(0, OWN, pack_state, 0)
    each_peer(lambda d: st_copy(d, True).start())
    loads[1].wait()
    for part in range(2):
        def pack_kv(i, _, part=part):
            for c in range(CAP):
                skv[part, i * CAP + c] = kvq[jnp.clip(rtab_s[i, 0, c], 0, 31), part]
            return 0

        lax.fori_loop(0, OWN, pack_kv, 0)
        each_peer(lambda d, part=part: kv_copy(part, d, True).start())
    for c in range(CAP):
        rst[b * CAP + c] = sst[b * CAP + c]
        for part in range(2):
            arrived[part][b * CAP + c] = skv[part, b * CAP + c]

    loads[4].wait()

    def end_tile(j, _):
        lanes = pl.ds(pl.multiple_of(j * LT, LT), LT)
        total = None
        for k in range(NCH):
            rows = slice(k * BQ, (k + 1) * BQ)
            xr = (x_v[rows, lanes].astype(F32) * dot(rem_v[rows, :], e2_v[:, lanes])).astype(BF16)
            part = dot(bt_v[:, rows], xr)
            if k < NCH - 1:
                l_v[k, :, lanes] = part
            total = part if k == 0 else thr_v[k : k + 1, lanes] * total + part
        lend_v[:, lanes] = total
        return 0

    lax.fori_loop(0, CH // LT, end_tile, 0)

    each_peer(lambda d: st_copy(d, False).wait_recv())

    def place(j, _):
        sta[pl.ds(pl.multiple_of(j * 16, 16), 16), :] = rst[jnp.clip(pos_s[1, j], 0, OWN * CAP - 1)]
        return 0

    lax.fori_loop(0, ENT, place, 0)
    r, c = iota((KEYS, KEYS), 0), iota((KEYS, KEYS), 1)
    order = jnp.where(c == ((r >> 1) & 7) * 64 + (r >> 4) * 2 + (r & 1), 1.0, 0.0).astype(BF16)
    sts[...] = dot(sta[...], order, ((0,), (0,))).astype(BF16)

    def sx_copy(q):
        return pltpu.make_async_remote_copy(
            src_ref=sts, dst_ref=inc.at[q], send_sem=sx_sem.at[0, 0], recv_sem=sx_sem.at[1, q],
            device_id=(0, b, m), device_id_type=MESH)

    @pl.when(s == 0)
    def _():
        inc[0] = sts[...]

    @pl.when(s > 0)
    def _():
        sx_copy(s).start()

    first = iota((BQ, BQ), 1) < 64

    def within(k, _):
        rows = pl.ds(pl.multiple_of(k * BQ, BQ), BQ)
        cum = cum_v[rows, :]
        cumt = cumt_v[pl.ds(pl.multiple_of(k * HEADS, HEADS), HEADS), :]
        g = g_v[k]
        for j in range(HEADS // 2):
            lanes = slice(j * 128, (j + 1) * 128)
            sides = []
            for h in (2 * j, 2 * j + 1):
                spread = cum[:, h : h + 1] - cumt[h : h + 1, :]
                sides.append((jnp.exp2(jnp.minimum(spread, 0.0)) * g).astype(BF16))
            xp = x_v[rows, lanes]
            zero = jnp.zeros_like(xp)
            both = jnp.concatenate([jnp.where(first, xp, zero), jnp.where(first, zero, xp)], axis=0)
            y_v[rows, lanes] = dot(jnp.concatenate(sides, axis=1), both)
        return 0

    lax.fori_loop(0, NCH, within, 0)

    def ag_copy(i, part, q, to):
        return pltpu.make_async_remote_copy(
            src_ref=kvall.at[q, part], dst_ref=kvall.at[q, part], send_sem=ag_sem.at[0, i], recv_sem=ag_sem.at[1, i],
            device_id=(to, b, m), device_id_type=MESH)

    def put_in_order(part):
        each_peer(lambda d: kv_copy(part, d, False).wait_recv())
        nothing = jnp.zeros((16, 2 * HD), BF16)

        def in_order(e, _):
            to = pl.ds(pl.multiple_of(e * 16, 16), 16)
            listed = e < cached[0]
            place_of = pos_s[0, e] if part else jnp.where(listed, pos_s[0, e], pos_s[0, 0])
            rows = arrived[part][jnp.clip(place_of, 0, OWN * CAP - 1)]
            kvall[s, part, to, :] = jnp.where(listed, rows, nothing) if part else rows
            return 0

        lax.fori_loop(0, ENT, in_order, 0)
        ag_copy(part, part, s, right).start()
        ag_copy(2 + part, part, s, left).start()

    def ch_copy(g):
        return pltpu.make_async_remote_copy(
            src_ref=snd.at[g], dst_ref=inc.at[g], send_sem=ch_sem.at[0, g], recv_sem=ch_sem.at[1, g],
            device_id=(lax.rem(s + 1, SEQ), b, m), device_id_type=MESH)

    def chain(who):
        @pl.when(s == who)
        def _():
            for g in range(SEQ):
                lanes = slice(g * KEYS, (g + 1) * KEYS)
                if who == 0 and g > 0:
                    sx_copy(g).wait_recv()
                if who > 0:
                    ch_copy(g).wait_recv()
                if who < SEQ - 1:
                    snd[g] = (thr_v[3:4, lanes] * inc[g].astype(F32) + lend_v[:, lanes]).astype(BF16)
                    ch_copy(g).start()

    loads[5].wait()
    for h in range(QH):
        qs_v[h] = high_low(q_v[:, h * HD : (h + 1) * HD].astype(F32) * SCALE2)
    m_v[...] = jnp.full(m_v.shape, NEGATIVE, F32)
    acc_v[...] = jnp.zeros(acc_v.shape, F32)

    def attend(key_ref, value_ref, change, weigh):
        def group(g, _):
            shared = pl.ds(pl.multiple_of(g * HD, HD), HD)
            keys = key_ref[:, shared]
            keys = jnp.concatenate([keys, keys], axis=1)
            values = value_ref[:, shared]
            values = jnp.concatenate([values, jnp.ones_like(values) if weigh is None else weigh[...]], axis=1)
            for i in range(4):
                scores = dot(qs_v[4 * g + i], keys, ((1,), (1,)))
                if change is not None:
                    scores = change(scores)
                before = m_v[g, i]
                now = jnp.maximum(before, jnp.max(scores, axis=1, keepdims=True))
                m_v[g, i] = now
                width = scores.shape[1] // 128
                probs = jnp.exp2(scores - jnp.concatenate([now] * width, axis=1)).astype(BF16)
                shrink = jnp.exp2(before - now)
                acc_v[g, i] = acc_v[g, i] * jnp.concatenate([shrink, shrink], axis=1) + dot(probs, values)
            return 0

        lax.fori_loop(0, QH // 4, group, 0, unroll=2)

    def causal(scores):
        return jnp.where(iota((T, T), 1) <= iota((T, T), 0), scores, NEGATIVE)

    nk_arrive(1, 1, 1)
    nk_arrive(0, 0, 1)
    for hop in onward:
        nk_send(*hop)
    chain(0)
    put_in_order(0)
    attend(nkv.at[s, 0], nkv.at[s, 1], causal, None)
    chain(1)
    put_in_order(1)
    chain(2)
    for hop in (hops[:3] + onward):
        nk_arrive(*hop)

    def earlier(j, _):
        attend(nkv.at[j, 0], nkv.at[j, 1], None, None)
        return 0

    lax.fori_loop(0, s, earlier, 0)
    weigh_v[...] = jnp.where(iota((KEYS, HD), 0) < cached[0] * 16, 1.0, 0.0).astype(BF16)
    attend(kvall.at[s, 0], kvall.at[s, 1], None, weigh_v)
    ag_copy(0, 0, left, right).wait_recv()
    ag_copy(4, 0, left, right).start()
    ag_copy(2, 0, right, left).wait_recv()
    ag_copy(3, 1, right, left).wait_recv()
    ag_copy(5, 1, right, left).start()
    ag_copy(1, 1, left, right).wait_recv()
    attend(kvall.at[left, 0], kvall.at[left, 1], None, weigh_v)
    attend(kvall.at[right, 0], kvall.at[right, 1], None, weigh_v)
    chain(3)

    loads[6].wait()

    def gate_tile(j, sums):
        lanes = pl.ds(pl.multiple_of(j * LT, LT), LT)
        state = inc[j // 2, :, pl.ds(pl.multiple_of((j % 2) * LT, LT), LT)].astype(F32)
        out = []
        for k in range(NCH):
            rows = slice(k * BQ, (k + 1) * BQ)
            carried = dot(c_ref[rows, :], state.astype(BF16)) * dot(ecx_v[rows, :], e2_v[:, lanes])
            y = y_v[rows, lanes] + carried + thr_v[4:5, lanes] * x_v[rows, lanes].astype(F32)
            z = z_v[rows, lanes].astype(F32)
            gated = y * (z / (1.0 + jnp.exp(-z)))
            y_v[rows, lanes] = gated
            square = gated * gated
            out.append(sums[k] + square[:, :128] + square[:, 128:])
            if k < NCH - 1:
                state = thr_v[k : k + 1, lanes] * state + l_v[k, :, lanes]
        return tuple(out)

    sums = lax.fori_loop(0, CH // LT, gate_tile, tuple(jnp.zeros((BQ, 128), F32) for _ in range(NCH)))
    ssx[m] = jnp.zeros((8, 128), F32)
    for k in range(NCH):
        ssx[m, k : k + 1, :] = jnp.sum(sums[k].T, axis=0, keepdims=True)

    def mp_copy(d, to):
        other = lax.rem(m + d, MPS) if to else lax.rem(m + MPS - d, MPS)
        at = m if to else other
        return pltpu.make_async_remote_copy(
            src_ref=ssx.at[at], dst_ref=ssx.at[at], send_sem=mp_sem.at[0, d], recv_sem=mp_sem.at[1, d],
            device_id=(s, b, other), device_id_type=MESH)

    for d in range(1, MPS):
        mp_copy(d, True).start()

    ag_copy(4, 0, across, right).wait_recv()
    ag_copy(5, 1, across, left).wait_recv()
    attend(kvall.at[across, 0], kvall.at[across, 1], None, weigh_v)

    def attn_out(h, _):
        at = pl.ds(pl.multiple_of(h * HD, HD), HD)
        both = acc_v[h // 4, h % 4]
        attn_ref[:, at] = (both[:, :HD] / both[:, HD:] * valid).astype(BF16)
        return 0

    lax.fori_loop(0, QH, attn_out, 0)

    for d in range(1, MPS):
        mp_copy(d, False).wait_recv()
    whole = ssx[0] + ssx[1] + ssx[2] + ssx[3]
    factor = lax.rsqrt(whole / (HEADS * 64 * MPS) + EPSILON)
    for k in range(NCH):
        rows = slice(k * BQ, (k + 1) * BQ)
        scale = jnp.broadcast_to(factor[k : k + 1], (BQ, BQ)).T * valid[rows]

        def norm_tile(j, _, rows=rows, scale=scale):
            lanes = pl.ds(pl.multiple_of(j * LT, LT), LT)
            ssm_ref[rows, lanes] = (y_v[rows, lanes] * jnp.concatenate([scale, scale], axis=1) * gain_ref[:, lanes]).astype(BF16)
            return 0

        lax.fori_loop(0, CH // LT, norm_tile, 0)

    each_peer(lambda d: tab_copy(d).wait_send())
    each_peer(lambda d: st_copy(d, True).wait_send())
    for part in range(2):
        each_peer(lambda d, part=part: kv_copy(part, d, True).wait_send())
    for who, slot, way in hops + onward:
        @pl.when(s == who)
        def _(slot=slot, way=way):
            nk_copy(slot, way).wait_send()

    @pl.when(s > 0)
    def _():
        sx_copy(s).wait_send()

    for part in range(2):
        ag_copy(part, part, s, right).wait_send()
        ag_copy(2 + part, part, s, left).wait_send()
    ag_copy(4, 0, left, right).wait_send()
    ag_copy(5, 1, right, left).wait_send()

    @pl.when(s < SEQ - 1)
    def _():
        for g in range(SEQ):
            ch_copy(g).wait_send()

    for d in range(1, MPS):
        mp_copy(d, True).wait_send()


def per_device(
    xs, gate_z, b_in, c_in, log_decay, d_skip, norm_gain, queries, keys_new, values_new,
    kv_pool, state_pool, new_len, cached_blocks, kv_owner, kv_slot, state_owner, state_slot,
):
    pieces = state_pool.reshape(state_pool.shape[0], 2 * HEADS, NS)
    vmem, smem = pl.BlockSpec(memory_space=pltpu.VMEM), pl.BlockSpec(memory_space=pltpu.SMEM)
    hbm = pl.BlockSpec(memory_space=pltpu.HBM)
    scratch = [
        pltpu.VMEM((T, CH), BF16),
        pltpu.VMEM((T, CH), BF16),
        pltpu.VMEM((T, QH * HD), BF16),
        pltpu.VMEM((SEQ, 2, T, 2 * HD), BF16),
        pltpu.VMEM((32, 2, 16, 2 * HD), BF16),
        pltpu.VMEM((64, 16, NS), BF16),
        pltpu.VMEM((OWN, 1, 128), I32),
        pltpu.VMEM((OWN, 1, 128), I32),
        pltpu.VMEM((8, 128), I32),
        pltpu.SMEM((OWN, 1, 128), I32),
        pltpu.SMEM((8, 128), I32),
        pltpu.VMEM((2, OWN * CAP, 16, 2 * HD), BF16),
        pltpu.VMEM((OWN * CAP, 16, 2 * HD), BF16),
        pltpu.VMEM((OWN * CAP, 16, 2 * HD), BF16),
        pltpu.VMEM((SEQ, 2, KEYS, 2 * HD), BF16),
        pltpu.VMEM((OWN * CAP, 16, NS), BF16),
        pltpu.VMEM((OWN * CAP, 16, NS), BF16),
        pltpu.VMEM((KEYS, NS), BF16),
        pltpu.VMEM((NS, KEYS), BF16),
        pltpu.VMEM((SEQ, NS, KEYS), BF16),
        pltpu.VMEM((SEQ, NS, KEYS), BF16),
        pltpu.VMEM((MPS, 8, 128), F32),
        pltpu.VMEM((T, HEADS), F32),
        pltpu.VMEM((NCH * HEADS, BQ), F32),
        pltpu.VMEM((T, 2 * HEADS), BF16),
        pltpu.VMEM((2 * HEADS, CH), BF16),
        pltpu.VMEM((16, CH), F32),
        pltpu.VMEM((NCH, BQ, BQ), F32),
        pltpu.VMEM((NS, T), BF16),
        pltpu.VMEM((T, 2 * HEADS), BF16),
        pltpu.VMEM((NCH - 1, NS, CH), F32),
        pltpu.VMEM((NS, CH), F32),
        pltpu.VMEM((T, CH), F32),
        pltpu.VMEM((QH, T, 2 * HD), BF16),
        pltpu.VMEM((KEYS, HD), BF16),
        pltpu.VMEM((2, QH // 2, T, 128), F32),
        pltpu.VMEM((2, QH // 2, T, 2 * HD), F32),
        pltpu.SemaphoreType.DMA((9,)),
        pltpu.SemaphoreType.DMA((2, OWN)),
        pltpu.SemaphoreType.DMA((2, 2, OWN)),
        pltpu.SemaphoreType.DMA((2, OWN)),
        pltpu.SemaphoreType.DMA((2, 6)),
        pltpu.SemaphoreType.DMA((2, SEQ, 2)),
        pltpu.SemaphoreType.DMA((2, SEQ)),
        pltpu.SemaphoreType.DMA((2, SEQ)),
        pltpu.SemaphoreType.DMA((2, MPS)),
    ]
    ssm, attn = pl.pallas_call(
        kernel,
        name="prefill",
        out_shape=(jax.ShapeDtypeStruct((T, CH), BF16), jax.ShapeDtypeStruct((T, QH * HD), BF16)),
        in_specs=[smem, smem] + [vmem] * 9 + [hbm] * 7,
        out_specs=(vmem, vmem),
        scratch_shapes=scratch,
        compiler_params=pltpu.CompilerParams(
            collective_id=0, has_side_effects=True, vmem_limit_bytes=56 * 1024 * 1024),
    )(
        new_len, cached_blocks, kv_owner[:, :, 0], kv_slot, state_owner[:, :, 0], state_slot,
        b_in[0], c_in[0], log_decay[0].T, d_skip.reshape(1, HEADS),
        norm_gain.reshape(1, CH), xs[0], gate_z[0], queries[0], keys_new[0], values_new[0], kv_pool, pieces,
    )
    return (ssm[None], attn[None])


def solution(mesh):
    in_specs = (
        P("batch", "seq", "mp"),
        P("batch", "seq", "mp"),
        P("batch", "seq", None),
        P("batch", "seq", None),
        P("batch", "seq", "mp"),
        P("mp"),
        P("mp"),
        P("batch", "seq", "mp"),
        P("batch", "seq", "mp"),
        P("batch", "seq", "mp"),
        P("batch", None, None, "mp"),
        P("batch", "mp", None, None),
        P("batch"),
        P("batch"),
        P("batch", None, None),
        P("batch", None),
        P("batch", None, None),
        P("batch", None),
    )
    out_specs = (P("batch", "seq", "mp"), P("batch", "seq", "mp"))
    return jax.shard_map(
        per_device, mesh=mesh, in_specs=in_specs, out_specs=out_specs, check_vma=False
    )
```

```python
import functools

import jax
import jax.numpy as jnp
from jax import lax
from jax.experimental import pallas as pl
from jax.experimental.pallas import tpu as pltpu
from jax.sharding import PartitionSpec as P

T = 384
CH = 2048
HEADS = 32
NS = 128
BQ = 128
NCH = T // BQ
CAP = 3
OWN = 16
SEQ = 4
MPS = 4
ENT = 32
QH = 8
HD = 128
KEYS = 512
LT = 256
EPSILON = 1e-05
NEGATIVE = -1e30
LOG2E = 1.4426950408889634
SCALE2 = HD ** (-0.5) * LOG2E
MESH = pl.DeviceIdType.MESH
F32, BF16, I32 = jnp.float32, jnp.bfloat16, jnp.int32


def iota(shape, dim):
    return lax.broadcasted_iota(I32, shape, dim)


def dot(a, b, dims=((1,), (0,)), precision=None):
    return lax.dot_general(
        a, b, (dims, ((), ())), precision=precision, preferred_element_type=F32
    )


def high_low(v):
    high = v.astype(BF16)
    return jnp.concatenate([high, (v - high.astype(F32)).astype(BF16)], axis=1)


def ranks_of(owner):
    lane, row = iota((ENT, ENT), 1), iota((ENT, ENT), 0)
    column = jnp.sum(jnp.where(lane == row, owner, 0), axis=1, keepdims=True)
    same = (column == owner) & (row < lane)
    return jnp.sum(jnp.where(same, 1, 0), axis=0, keepdims=True)


def kernel(
    new_len, cached, ko_ref, kl_ref, so_ref, sl_ref, b_ref, c_ref, ld_ref, dsk_ref, gain_ref,
    x_hbm, z_hbm, q_hbm, k_hbm, v_hbm, kvp_hbm, stp_hbm,
    ssm_ref, attn_ref,
    x_v, z_v, q_v, nkv, kvq, stq, tab_v, rtab_v, pos_v, rtab_s, pos_s,
    skv, rk, rv, kvall, sst, rst, sta, sts, inc, snd, ssx,
    cum_v, cumt_v, ecx_v, e2_v, thr_v, g_v, bt_v, rem_v, l_v, lend_v, y_v, qs_v, weigh_v, m_v, acc_v,
    load_sem, tab_sem, z_sem, st_sem, ag_sem, nk_sem, sx_sem, ch_sem, mp_sem,
):
    arrived = (rk, rv)
    s, b, m = lax.axis_index("seq"), lax.axis_index("batch"), lax.axis_index("mp")

    quarter = pl.ds(pl.multiple_of(s * 16, 16), 16)
    loads = [
        pltpu.make_async_copy(stp_hbm.at[:, quarter, :], stq, load_sem.at[0]),
        pltpu.make_async_copy(kvp_hbm.at[:, :, quarter, :], kvq, load_sem.at[1]),
        pltpu.make_async_copy(k_hbm, nkv.at[s, 0], load_sem.at[2]),
        pltpu.make_async_copy(v_hbm, nkv.at[s, 1], load_sem.at[3]),
        pltpu.make_async_copy(x_hbm, x_v, load_sem.at[4]),
        pltpu.make_async_copy(q_hbm, q_v, load_sem.at[5]),
        pltpu.make_async_copy(z_hbm, z_v, load_sem.at[6]),
    ]
    for load in loads:
        load.start()

    barrier = pltpu.get_barrier_semaphore()

    def greet(d, _):
        pl.semaphore_signal(barrier, inc=1, device_id=(s, lax.rem(b + d, OWN), m), device_id_type=MESH)
        return 0

    lax.fori_loop(1, OWN, greet, 0)
    for d in range(1, SEQ):
        pl.semaphore_signal(barrier, inc=1, device_id=(lax.rem(s + d, SEQ), b, m), device_id_type=MESH)
    for d in range(1, MPS):
        pl.semaphore_signal(barrier, inc=1, device_id=(s, b, lax.rem(m + d, MPS)), device_id_type=MESH)

    lane16, row16 = iota((OWN, 128), 1), iota((OWN, ENT), 0)
    table = jnp.zeros((OWN, 128), I32)
    for part, (owner_ref, slot_ref) in enumerate(((ko_ref, kl_ref), (so_ref, sl_ref))):
        owner, slot = owner_ref[...], slot_ref[...]
        rank = ranks_of(owner)
        pos_v[part : part + 1, :ENT] = jnp.clip(owner * CAP + rank, 0, OWN * CAP - 1)
        for c in range(CAP):
            hit = (owner == row16) & (rank == c)
            asked = jnp.sum(jnp.where(hit, slot, 0), axis=1, keepdims=True)
            table = jnp.where(lane16 == part * CAP + c, asked, table)
    for o in range(OWN):
        tab_v[o] = table[o : o + 1]
    rtab_v[b] = tab_v[b]
    to_pos = pltpu.make_async_copy(pos_v, pos_s, load_sem.at[7])
    to_pos.start()

    pl.semaphore_wait(barrier, OWN - 1 + SEQ - 1 + MPS - 1)

    def tab_copy(d):
        peer = lax.rem(b + d, OWN)
        return pltpu.make_async_remote_copy(
            src_ref=tab_v.at[peer], dst_ref=rtab_v.at[b], send_sem=tab_sem.at[0, d], recv_sem=tab_sem.at[1, d],
            device_id=(s, peer, m), device_id_type=MESH)

    def tab_from(d):
        source = lax.rem(b + OWN - d, OWN)
        return pltpu.make_async_remote_copy(
            src_ref=tab_v.at[source], dst_ref=rtab_v.at[source], send_sem=tab_sem.at[0, d], recv_sem=tab_sem.at[1, d],
            device_id=(s, source, m), device_id_type=MESH)

    def st_copy(d, to):
        peer = lax.rem(b + d, OWN) if to else lax.rem(b + OWN - d, OWN)
        at = b if to else peer
        return pltpu.make_async_remote_copy(
            src_ref=sst.at[pl.ds(peer * CAP, CAP)], dst_ref=rst.at[pl.ds(at * CAP, CAP)],
            send_sem=st_sem.at[0, d], recv_sem=st_sem.at[1, d], device_id=(s, peer, m), device_id_type=MESH)

    def kv_copy(part, d, to):
        peer = lax.rem(b + d, OWN) if to else lax.rem(b + OWN - d, OWN)
        at = b if to else peer
        return pltpu.make_async_remote_copy(
            src_ref=skv.at[part, pl.ds(peer * CAP, CAP)], dst_ref=arrived[part].at[pl.ds(at * CAP, CAP)],
            send_sem=z_sem.at[0, part, d], recv_sem=z_sem.at[1, part, d], device_id=(s, peer, m), device_id_type=MESH)

    def each_peer(act):
        def one(d, _):
            act(d)
            return 0

        lax.fori_loop(1, OWN, one, 0)

    each_peer(lambda d: tab_copy(d).start())

    loads[2].wait()
    loads[3].wait()

    right, left = lax.rem(s + 1, SEQ), lax.rem(s + SEQ - 1, SEQ)
    across = lax.rem(s + 2, SEQ)

    def nk_copy(slot, way):
        return pltpu.make_async_remote_copy(
            src_ref=nkv.at[slot], dst_ref=nkv.at[slot], send_sem=nk_sem.at[0, slot, way], recv_sem=nk_sem.at[1, slot, way],
            device_id=(left if way else right, b, m), device_id_type=MESH)

    hops = ((0, 0, 0), (1, 1, 0), (2, 2, 0), (1, 1, 1), (0, 0, 1))
    onward = ((0, 1, 1), (3, 0, 1))

    def nk_send(who, slot, way):
        @pl.when(s == who)
        def _():
            nk_copy(slot, way).start()

    def nk_arrive(who, slot, way):
        @pl.when(s == (who + SEQ - 1 if way else who + 1) % SEQ)
        def _():
            nk_copy(slot, way).wait_recv()

    for hop in hops:
        nk_send(*hop)

    tri = jnp.where(iota((BQ, BQ), 0) >= iota((BQ, BQ), 1), 1.0, 0.0)
    triu = jnp.where(iota((BQ, BQ), 0) <= iota((BQ, BQ), 1), 1.0, 0.0)
    valid = jnp.where(s * T + iota((T, 1), 0) < new_len[0], 1.0, 0.0)
    valid_row = jnp.where(s * T + iota((1, T), 1) < new_len[0], 1.0, 0.0)
    e2_v[...] = jnp.where((iota((2 * HEADS, CH), 0) & (HEADS - 1)) == (iota((2 * HEADS, CH), 1) >> 6), 1.0, 0.0).astype(BF16)
    totals = []
    for k in range(NCH):
        rows = slice(k * BQ, (k + 1) * BQ)
        dec = ld_ref[:, rows] * valid_row[:, rows]
        cum = dot(tri, dec, ((1,), (1,)), lax.Precision.HIGHEST)
        cumt_v[k * HEADS : (k + 1) * HEADS, :] = LOG2E * dot(dec, triu, precision=lax.Precision.HIGHEST)
        cum_v[rows, :] = LOG2E * cum
        total = cum[BQ - 1 : BQ]
        totals.append(total)
        ecx_v[rows, :] = high_low(jnp.exp(cum))
        rem_v[rows, :] = high_low(jnp.exp(total - cum) * valid[rows])
        bt_v[:, rows] = b_ref[rows, :].astype(F32).T.astype(BF16)
        g = dot(c_ref[rows, :], b_ref[rows, :], ((1,), (1,)))
        g_v[k] = g * tri
    row = iota((16, HEADS), 0)
    small = jnp.where(row == 3, jnp.exp(totals[0] + totals[1] + totals[2]), jnp.where(row == 4, dsk_ref[...], 0.0))
    for k in range(NCH):
        small = jnp.where(row == k, jnp.exp(totals[k]), small)
    thr_v[...] = dot(high_low(small), e2_v[...])

    each_peer(lambda d: tab_from(d).wait_recv())
    to_tab = pltpu.make_async_copy(rtab_v, rtab_s, load_sem.at[8])
    to_tab.start()
    to_tab.wait()
    to_pos.wait()
    loads[0].wait()

    def pack_state(i, _):
        for c in range(CAP):
            sst[i * CAP + c] = stq[jnp.clip(rtab_s[i, 0, CAP + c], 0, 63)]
        return 0

    lax.fori_loop(0, OWN, pack_state, 0)
    each_peer(lambda d: st_copy(d, True).start())
    loads[1].wait()
    for part in range(2):
        def pack_kv(i, _, part=part):
            for c in range(CAP):
                skv[part, i * CAP + c] = kvq[jnp.clip(rtab_s[i, 0, c], 0, 31), part]
            return 0

        lax.fori_loop(0, OWN, pack_kv, 0)
        each_peer(lambda d, part=part: kv_copy(part, d, True).start())
    for c in range(CAP):
        rst[b * CAP + c] = sst[b * CAP + c]
        for part in range(2):
            arrived[part][b * CAP + c] = skv[part, b * CAP + c]

    loads[4].wait()

    def end_tile(j, _):
        lanes = pl.ds(pl.multiple_of(j * LT, LT), LT)
        total = None
        for k in range(NCH):
            rows = slice(k * BQ, (k + 1) * BQ)
            xr = (x_v[rows, lanes].astype(F32) * dot(rem_v[rows, :], e2_v[:, lanes])).astype(BF16)
            part = dot(bt_v[:, rows], xr)
            if k < NCH - 1:
                l_v[k, :, lanes] = part
            total = part if k == 0 else thr_v[k : k + 1, lanes] * total + part
        lend_v[:, lanes] = total
        return 0

    lax.fori_loop(0, CH // LT, end_tile, 0)

    each_peer(lambda d: st_copy(d, False).wait_recv())

    def place(j, _):
        sta[pl.ds(pl.multiple_of(j * 16, 16), 16), :] = rst[jnp.clip(pos_s[1, j], 0, OWN * CAP - 1)]
        return 0

    lax.fori_loop(0, ENT, place, 0)
    r, c = iota((KEYS, KEYS), 0), iota((KEYS, KEYS), 1)
    order = jnp.where(c == ((r >> 1) & 7) * 64 + (r >> 4) * 2 + (r & 1), 1.0, 0.0).astype(BF16)
    sts[...] = dot(sta[...], order, ((0,), (0,))).astype(BF16)

    def sx_copy(q):
        return pltpu.make_async_remote_copy(
            src_ref=sts, dst_ref=inc.at[q], send_sem=sx_sem.at[0, 0], recv_sem=sx_sem.at[1, q],
            device_id=(0, b, m), device_id_type=MESH)

    @pl.when(s == 0)
    def _():
        inc[0] = sts[...]

    @pl.when(s > 0)
    def _():
        sx_copy(s).start()

    first = iota((BQ, BQ), 1) < 64

    def within(k, _):
        rows = pl.ds(pl.multiple_of(k * BQ, BQ), BQ)
        cum = cum_v[rows, :]
        cumt = cumt_v[pl.ds(pl.multiple_of(k * HEADS, HEADS), HEADS), :]
        g = g_v[k]
        for j in range(HEADS // 2):
            lanes = slice(j * 128, (j + 1) * 128)
            sides = []
            for h in (2 * j, 2 * j + 1):
                spread = cum[:, h : h + 1] - cumt[h : h + 1, :]
                sides.append((jnp.exp2(jnp.minimum(spread, 0.0)) * g).astype(BF16))
            xp = x_v[rows, lanes]
            zero = jnp.zeros_like(xp)
            both = jnp.concatenate([jnp.where(first, xp, zero), jnp.where(first, zero, xp)], axis=0)
            y_v[rows, lanes] = dot(jnp.concatenate(sides, axis=1), both)
        return 0

    lax.fori_loop(0, NCH, within, 0)

    def ag_copy(i, part, q, to):
        return pltpu.make_async_remote_copy(
            src_ref=kvall.at[q, part], dst_ref=kvall.at[q, part], send_sem=ag_sem.at[0, i], recv_sem=ag_sem.at[1, i],
            device_id=(to, b, m), device_id_type=MESH)

    def put_in_order(part):
        each_peer(lambda d: kv_copy(part, d, False).wait_recv())
        nothing = jnp.zeros((16, 2 * HD), BF16)

        def in_order(e, _):
            to = pl.ds(pl.multiple_of(e * 16, 16), 16)
            listed = e < cached[0]
            place_of = pos_s[0, e] if part else jnp.where(listed, pos_s[0, e], pos_s[0, 0])
            rows = arrived[part][jnp.clip(place_of, 0, OWN * CAP - 1)]
            kvall[s, part, to, :] = jnp.where(listed, rows, nothing) if part else rows
            return 0

        lax.fori_loop(0, ENT, in_order, 0)
        ag_copy(part, part, s, right).start()
        ag_copy(2 + part, part, s, left).start()

    def ch_copy(g):
        return pltpu.make_async_remote_copy(
            src_ref=snd.at[g], dst_ref=inc.at[g], send_sem=ch_sem.at[0, g], recv_sem=ch_sem.at[1, g],
            device_id=(lax.rem(s + 1, SEQ), b, m), device_id_type=MESH)

    def chain(who):
        @pl.when(s == who)
        def _():
            for g in range(SEQ):
                lanes = slice(g * KEYS, (g + 1) * KEYS)
                if who == 0 and g > 0:
                    sx_copy(g).wait_recv()
                if who > 0:
                    ch_copy(g).wait_recv()
                if who < SEQ - 1:
                    snd[g] = (thr_v[3:4, lanes] * inc[g].astype(F32) + lend_v[:, lanes]).astype(BF16)
                    ch_copy(g).start()

    loads[5].wait()
    for h in range(QH):
        qs_v[h] = high_low(q_v[:, h * HD : (h + 1) * HD].astype(F32) * SCALE2)
    m_v[...] = jnp.full(m_v.shape, NEGATIVE, F32)
    acc_v[...] = jnp.zeros(acc_v.shape, F32)

    def attend(key_ref, value_ref, change, weigh):
        def group(g, _):
            shared = pl.ds(pl.multiple_of(g * HD, HD), HD)
            keys = key_ref[:, shared]
            keys = jnp.concatenate([keys, keys], axis=1)
            values = value_ref[:, shared]
            values = jnp.concatenate([values, jnp.ones_like(values) if weigh is None else weigh[...]], axis=1)
            for i in range(4):
                scores = dot(qs_v[4 * g + i], keys, ((1,), (1,)))
                if change is not None:
                    scores = change(scores)
                before = m_v[g, i]
                now = jnp.maximum(before, jnp.max(scores, axis=1, keepdims=True))
                m_v[g, i] = now
                width = scores.shape[1] // 128
                probs = jnp.exp2(scores - jnp.concatenate([now] * width, axis=1)).astype(BF16)
                shrink = jnp.exp2(before - now)
                acc_v[g, i] = acc_v[g, i] * jnp.concatenate([shrink, shrink], axis=1) + dot(probs, values)
            return 0

        lax.fori_loop(0, QH // 4, group, 0, unroll=2)

    def causal(scores):
        return jnp.where(iota((T, T), 1) <= iota((T, T), 0), scores, NEGATIVE)

    nk_arrive(1, 1, 1)
    nk_arrive(0, 0, 1)
    for hop in onward:
        nk_send(*hop)
    chain(0)
    put_in_order(0)
    attend(nkv.at[s, 0], nkv.at[s, 1], causal, None)
    chain(1)
    put_in_order(1)
    chain(2)
    for hop in (hops[:3] + onward):
        nk_arrive(*hop)

    def earlier(j, _):
        attend(nkv.at[j, 0], nkv.at[j, 1], None, None)
        return 0

    lax.fori_loop(0, s, earlier, 0)
    weigh_v[...] = jnp.where(iota((KEYS, HD), 0) < cached[0] * 16, 1.0, 0.0).astype(BF16)
    attend(kvall.at[s, 0], kvall.at[s, 1], None, weigh_v)
    ag_copy(0, 0, left, right).wait_recv()
    ag_copy(4, 0, left, right).start()
    ag_copy(2, 0, right, left).wait_recv()
    ag_copy(3, 1, right, left).wait_recv()
    ag_copy(5, 1, right, left).start()
    ag_copy(1, 1, left, right).wait_recv()
    attend(kvall.at[left, 0], kvall.at[left, 1], None, weigh_v)
    attend(kvall.at[right, 0], kvall.at[right, 1], None, weigh_v)
    chain(3)

    loads[6].wait()

    def gate_tile(j, sums):
        lanes = pl.ds(pl.multiple_of(j * LT, LT), LT)
        state = inc[j // 2, :, pl.ds(pl.multiple_of((j % 2) * LT, LT), LT)].astype(F32)
        out = []
        for k in range(NCH):
            rows = slice(k * BQ, (k + 1) * BQ)
            carried = dot(c_ref[rows, :], state.astype(BF16)) * dot(ecx_v[rows, :], e2_v[:, lanes])
            y = y_v[rows, lanes] + carried + thr_v[4:5, lanes] * x_v[rows, lanes].astype(F32)
            z = z_v[rows, lanes].astype(F32)
            gated = y * (z / (1.0 + jnp.exp(-z)))
            y_v[rows, lanes] = gated
            square = gated * gated
            out.append(sums[k] + square[:, :128] + square[:, 128:])
            if k < NCH - 1:
                state = thr_v[k : k + 1, lanes] * state + l_v[k, :, lanes]
        return tuple(out)

    sums = lax.fori_loop(0, CH // LT, gate_tile, tuple(jnp.zeros((BQ, 128), F32) for _ in range(NCH)))
    ssx[m] = jnp.zeros((8, 128), F32)
    for k in range(NCH):
        ssx[m, k : k + 1, :] = jnp.sum(sums[k].T, axis=0, keepdims=True)

    def mp_copy(d, to):
        other = lax.rem(m + d, MPS) if to else lax.rem(m + MPS - d, MPS)
        at = m if to else other
        return pltpu.make_async_remote_copy(
            src_ref=ssx.at[at], dst_ref=ssx.at[at], send_sem=mp_sem.at[0, d], recv_sem=mp_sem.at[1, d],
            device_id=(s, b, other), device_id_type=MESH)

    for d in range(1, MPS):
        mp_copy(d, True).start()

    ag_copy(4, 0, across, right).wait_recv()
    ag_copy(5, 1, across, left).wait_recv()
    attend(kvall.at[across, 0], kvall.at[across, 1], None, weigh_v)

    def attn_out(h, _):
        at = pl.ds(pl.multiple_of(h * HD, HD), HD)
        both = acc_v[h // 4, h % 4]
        attn_ref[:, at] = (both[:, :HD] / both[:, HD:] * valid).astype(BF16)
        return 0

    lax.fori_loop(0, QH, attn_out, 0)

    for d in range(1, MPS):
        mp_copy(d, False).wait_recv()
    whole = ssx[0] + ssx[1] + ssx[2] + ssx[3]
    factor = lax.rsqrt(whole / (HEADS * 64 * MPS) + EPSILON)
    for k in range(NCH):
        rows = slice(k * BQ, (k + 1) * BQ)
        scale = jnp.broadcast_to(factor[k : k + 1], (BQ, BQ)).T * valid[rows]

        def norm_tile(j, _, rows=rows, scale=scale):
            lanes = pl.ds(pl.multiple_of(j * LT, LT), LT)
            ssm_ref[rows, lanes] = (y_v[rows, lanes] * jnp.concatenate([scale, scale], axis=1) * gain_ref[:, lanes]).astype(BF16)
            return 0

        lax.fori_loop(0, CH // LT, norm_tile, 0)

    each_peer(lambda d: tab_copy(d).wait_send())
    each_peer(lambda d: st_copy(d, True).wait_send())
    for part in range(2):
        each_peer(lambda d, part=part: kv_copy(part, d, True).wait_send())
    for who, slot, way in hops + onward:
        @pl.when(s == who)
        def _(slot=slot, way=way):
            nk_copy(slot, way).wait_send()

    @pl.when(s > 0)
    def _():
        sx_copy(s).wait_send()

    for part in range(2):
        ag_copy(part, part, s, right).wait_send()
        ag_copy(2 + part, part, s, left).wait_send()
    ag_copy(4, 0, left, right).wait_send()
    ag_copy(5, 1, right, left).wait_send()

    @pl.when(s < SEQ - 1)
    def _():
        for g in range(SEQ):
            ch_copy(g).wait_send()

    for d in range(1, MPS):
        mp_copy(d, True).wait_send()


def per_device(
    xs, gate_z, b_in, c_in, log_decay, d_skip, norm_gain, queries, keys_new, values_new,
    kv_pool, state_pool, new_len, cached_blocks, kv_owner, kv_slot, state_owner, state_slot,
):
    pieces = state_pool.reshape(state_pool.shape[0], 2 * HEADS, NS)
    vmem, smem = pl.BlockSpec(memory_space=pltpu.VMEM), pl.BlockSpec(memory_space=pltpu.SMEM)
    hbm = pl.BlockSpec(memory_space=pltpu.HBM)
    scratch = [
        pltpu.VMEM((T, CH), BF16),
        pltpu.VMEM((T, CH), BF16),
        pltpu.VMEM((T, QH * HD), BF16),
        pltpu.VMEM((SEQ, 2, T, 2 * HD), BF16),
        pltpu.VMEM((32, 2, 16, 2 * HD), BF16),
        pltpu.VMEM((64, 16, NS), BF16),
        pltpu.VMEM((OWN, 1, 128), I32),
        pltpu.VMEM((OWN, 1, 128), I32),
        pltpu.VMEM((8, 128), I32),
        pltpu.SMEM((OWN, 1, 128), I32),
        pltpu.SMEM((8, 128), I32),
        pltpu.VMEM((2, OWN * CAP, 16, 2 * HD), BF16),
        pltpu.VMEM((OWN * CAP, 16, 2 * HD), BF16),
        pltpu.VMEM((OWN * CAP, 16, 2 * HD), BF16),
        pltpu.VMEM((SEQ, 2, KEYS, 2 * HD), BF16),
        pltpu.VMEM((OWN * CAP, 16, NS), BF16),
        pltpu.VMEM((OWN * CAP, 16, NS), BF16),
        pltpu.VMEM((KEYS, NS), BF16),
        pltpu.VMEM((NS, KEYS), BF16),
        pltpu.VMEM((SEQ, NS, KEYS), BF16),
        pltpu.VMEM((SEQ, NS, KEYS), BF16),
        pltpu.VMEM((MPS, 8, 128), F32),
        pltpu.VMEM((T, HEADS), F32),
        pltpu.VMEM((NCH * HEADS, BQ), F32),
        pltpu.VMEM((T, 2 * HEADS), BF16),
        pltpu.VMEM((2 * HEADS, CH), BF16),
        pltpu.VMEM((16, CH), F32),
        pltpu.VMEM((NCH, BQ, BQ), F32),
        pltpu.VMEM((NS, T), BF16),
        pltpu.VMEM((T, 2 * HEADS), BF16),
        pltpu.VMEM((NCH - 1, NS, CH), F32),
        pltpu.VMEM((NS, CH), F32),
        pltpu.VMEM((T, CH), F32),
        pltpu.VMEM((QH, T, 2 * HD), BF16),
        pltpu.VMEM((KEYS, HD), BF16),
        pltpu.VMEM((2, QH // 2, T, 128), F32),
        pltpu.VMEM((2, QH // 2, T, 2 * HD), F32),
        pltpu.SemaphoreType.DMA((9,)),
        pltpu.SemaphoreType.DMA((2, OWN)),
        pltpu.SemaphoreType.DMA((2, 2, OWN)),
        pltpu.SemaphoreType.DMA((2, OWN)),
        pltpu.SemaphoreType.DMA((2, 6)),
        pltpu.SemaphoreType.DMA((2, SEQ, 2)),
        pltpu.SemaphoreType.DMA((2, SEQ)),
        pltpu.SemaphoreType.DMA((2, SEQ)),
        pltpu.SemaphoreType.DMA((2, MPS)),
    ]
    ssm, attn = pl.pallas_call(
        kernel,
        name="prefill",
        out_shape=(jax.ShapeDtypeStruct((T, CH), BF16), jax.ShapeDtypeStruct((T, QH * HD), BF16)),
        in_specs=[smem, smem] + [vmem] * 9 + [hbm] * 7,
        out_specs=(vmem, vmem),
        scratch_shapes=scratch,
        compiler_params=pltpu.CompilerParams(
            collective_id=0, has_side_effects=True, vmem_limit_bytes=44 * 1024 * 1024),
    )(
        new_len, cached_blocks,
        *(pltpu.with_memory_space_constraint(value, pltpu.HBM) for value in (
            kv_owner[:, :, 0], kv_slot, state_owner[:, :, 0], state_slot,
            b_in[0], c_in[0], log_decay[0].T, d_skip.reshape(1, HEADS), norm_gain.reshape(1, CH),
            xs[0], gate_z[0], queries[0], keys_new[0], values_new[0], kv_pool, pieces,
        )),
    )
    return (ssm[None], attn[None])


def solution(mesh):
    in_specs = (
        P("batch", "seq", "mp"),
        P("batch", "seq", "mp"),
        P("batch", "seq", None),
        P("batch", "seq", None),
        P("batch", "seq", "mp"),
        P("mp"),
        P("mp"),
        P("batch", "seq", "mp"),
        P("batch", "seq", "mp"),
        P("batch", "seq", "mp"),
        P("batch", None, None, "mp"),
        P("batch", "mp", None, None),
        P("batch"),
        P("batch"),
        P("batch", None, None),
        P("batch", None),
        P("batch", None, None),
        P("batch", None),
    )
    out_specs = (P("batch", "seq", "mp"), P("batch", "seq", "mp"))
    return jax.shard_map(
        per_device, mesh=mesh, in_specs=in_specs, out_specs=out_specs, check_vma=False
    )
```

```python
import functools

import jax
import jax.numpy as jnp
from jax import lax
from jax.experimental import pallas as pl
from jax.experimental.pallas import tpu as pltpu
from jax.sharding import PartitionSpec as P

T = 384
CH = 2048
HEADS = 32
NS = 128
BQ = 128
NCH = T // BQ
CAP = 3
OWN = 16
SEQ = 4
MPS = 4
ENT = 32
QH = 8
HD = 128
KEYS = 512
LT = 256
EPSILON = 1e-05
NEGATIVE = -1e30
LOG2E = 1.4426950408889634
SCALE2 = HD ** (-0.5) * LOG2E
MESH = pl.DeviceIdType.MESH
F32, BF16, I32 = jnp.float32, jnp.bfloat16, jnp.int32


def iota(shape, dim):
    return lax.broadcasted_iota(I32, shape, dim)


def dot(a, b, dims=((1,), (0,)), precision=None):
    return lax.dot_general(
        a, b, (dims, ((), ())), precision=precision, preferred_element_type=F32
    )


def high_low(v):
    high = v.astype(BF16)
    return jnp.concatenate([high, (v - high.astype(F32)).astype(BF16)], axis=1)


def ranks_of(owner):
    lane, row = iota((ENT, ENT), 1), iota((ENT, ENT), 0)
    column = jnp.sum(jnp.where(lane == row, owner, 0), axis=1, keepdims=True)
    same = (column == owner) & (row < lane)
    return jnp.sum(jnp.where(same, 1, 0), axis=0, keepdims=True)


def kernel(
    new_len, cached, ko_ref, kl_ref, so_ref, sl_ref, b_ref, c_ref, ld_ref, dsk_ref, gain_ref,
    x_hbm, z_hbm, q_hbm, k_hbm, v_hbm, kvp_hbm, stp_hbm,
    ssm_ref, attn_ref,
    x_v, z_v, q_v, nkv, kvq, stq, tab_v, rtab_v, pos_v, rtab_s, pos_s,
    skv, rk, rv, kvall, sst, rst, sta, sts, inc, snd, ssx,
    cum_v, cumt_v, ecx_v, e2_v, thr_v, g_v, bt_v, rem_v, l_v, lend_v, y_v, qs_v, weigh_v, m_v, acc_v,
    load_sem, tab_sem, z_sem, st_sem, ag_sem, nk_sem, sx_sem, ch_sem, mp_sem,
):
    arrived = (rk, rv)
    s, b, m = lax.axis_index("seq"), lax.axis_index("batch"), lax.axis_index("mp")

    quarter = pl.ds(pl.multiple_of(s * 16, 16), 16)
    loads = [
        pltpu.make_async_copy(stp_hbm.at[:, quarter, :], stq, load_sem.at[0]),
        pltpu.make_async_copy(kvp_hbm.at[:, :, quarter, :], kvq, load_sem.at[1]),
        pltpu.make_async_copy(k_hbm, nkv.at[s, 0], load_sem.at[2]),
        pltpu.make_async_copy(v_hbm, nkv.at[s, 1], load_sem.at[3]),
        pltpu.make_async_copy(x_hbm, x_v, load_sem.at[4]),
        pltpu.make_async_copy(q_hbm, q_v, load_sem.at[5]),
        pltpu.make_async_copy(z_hbm, z_v, load_sem.at[6]),
    ]
    for load in loads:
        load.start()

    barrier = pltpu.get_barrier_semaphore()

    def greet(d, _):
        pl.semaphore_signal(barrier, inc=1, device_id=(s, lax.rem(b + d, OWN), m), device_id_type=MESH)
        return 0

    lax.fori_loop(1, OWN, greet, 0)
    for d in range(1, SEQ):
        pl.semaphore_signal(barrier, inc=1, device_id=(lax.rem(s + d, SEQ), b, m), device_id_type=MESH)
    for d in range(1, MPS):
        pl.semaphore_signal(barrier, inc=1, device_id=(s, b, lax.rem(m + d, MPS)), device_id_type=MESH)

    lane16, row16 = iota((OWN, 128), 1), iota((OWN, ENT), 0)
    table = jnp.zeros((OWN, 128), I32)
    for part, (owner_ref, slot_ref) in enumerate(((ko_ref, kl_ref), (so_ref, sl_ref))):
        owner, slot = owner_ref[...], slot_ref[...]
        rank = ranks_of(owner)
        pos_v[part : part + 1, :ENT] = jnp.clip(owner * CAP + rank, 0, OWN * CAP - 1)
        for c in range(CAP):
            hit = (owner == row16) & (rank == c)
            asked = jnp.sum(jnp.where(hit, slot, 0), axis=1, keepdims=True)
            table = jnp.where(lane16 == part * CAP + c, asked, table)
    for o in range(OWN):
        tab_v[o] = table[o : o + 1]
    rtab_v[b] = tab_v[b]
    to_pos = pltpu.make_async_copy(pos_v, pos_s, load_sem.at[7])
    to_pos.start()

    pl.semaphore_wait(barrier, OWN - 1 + SEQ - 1 + MPS - 1)

    def tab_copy(d):
        peer = lax.rem(b + d, OWN)
        return pltpu.make_async_remote_copy(
            src_ref=tab_v.at[peer], dst_ref=rtab_v.at[b], send_sem=tab_sem.at[0, d], recv_sem=tab_sem.at[1, d],
            device_id=(s, peer, m), device_id_type=MESH)

    def tab_from(d):
        source = lax.rem(b + OWN - d, OWN)
        return pltpu.make_async_remote_copy(
            src_ref=tab_v.at[source], dst_ref=rtab_v.at[source], send_sem=tab_sem.at[0, d], recv_sem=tab_sem.at[1, d],
            device_id=(s, source, m), device_id_type=MESH)

    def st_copy(d, to):
        peer = lax.rem(b + d, OWN) if to else lax.rem(b + OWN - d, OWN)
        at = b if to else peer
        return pltpu.make_async_remote_copy(
            src_ref=sst.at[pl.ds(peer * CAP, CAP)], dst_ref=rst.at[pl.ds(at * CAP, CAP)],
            send_sem=st_sem.at[0, d], recv_sem=st_sem.at[1, d], device_id=(s, peer, m), device_id_type=MESH)

    def kv_copy(part, d, to):
        peer = lax.rem(b + d, OWN) if to else lax.rem(b + OWN - d, OWN)
        at = b if to else peer
        return pltpu.make_async_remote_copy(
            src_ref=skv.at[part, pl.ds(peer * CAP, CAP)], dst_ref=arrived[part].at[pl.ds(at * CAP, CAP)],
            send_sem=z_sem.at[0, part, d], recv_sem=z_sem.at[1, part, d], device_id=(s, peer, m), device_id_type=MESH)

    def each_peer(act):
        def one(d, _):
            act(d)
            return 0

        lax.fori_loop(1, OWN, one, 0)

    each_peer(lambda d: tab_copy(d).start())

    loads[2].wait()
    loads[3].wait()

    right, left = lax.rem(s + 1, SEQ), lax.rem(s + SEQ - 1, SEQ)
    across = lax.rem(s + 2, SEQ)

    def nk_copy(slot, way):
        return pltpu.make_async_remote_copy(
            src_ref=nkv.at[slot], dst_ref=nkv.at[slot], send_sem=nk_sem.at[0, slot, way], recv_sem=nk_sem.at[1, slot, way],
            device_id=(left if way else right, b, m), device_id_type=MESH)

    hops = ((0, 0, 0), (1, 1, 0), (2, 2, 0), (1, 1, 1), (0, 0, 1))
    onward = ((0, 1, 1), (3, 0, 1))

    def nk_send(who, slot, way):
        @pl.when(s == who)
        def _():
            nk_copy(slot, way).start()

    def nk_arrive(who, slot, way):
        @pl.when(s == (who + SEQ - 1 if way else who + 1) % SEQ)
        def _():
            nk_copy(slot, way).wait_recv()

    for hop in hops:
        nk_send(*hop)

    tri = jnp.where(iota((BQ, BQ), 0) >= iota((BQ, BQ), 1), 1.0, 0.0)
    triu = jnp.where(iota((BQ, BQ), 0) <= iota((BQ, BQ), 1), 1.0, 0.0)
    valid = jnp.where(s * T + iota((T, 1), 0) < new_len[0], 1.0, 0.0)
    valid_row = jnp.where(s * T + iota((1, T), 1) < new_len[0], 1.0, 0.0)
    e2_v[...] = jnp.where((iota((2 * HEADS, CH), 0) & (HEADS - 1)) == (iota((2 * HEADS, CH), 1) >> 6), 1.0, 0.0).astype(BF16)
    totals = []
    for k in range(NCH):
        rows = slice(k * BQ, (k + 1) * BQ)
        dec = ld_ref[:, rows] * valid_row[:, rows]
        cum = dot(tri, dec, ((1,), (1,)), lax.Precision.HIGHEST)
        cumt_v[k * HEADS : (k + 1) * HEADS, :] = LOG2E * dot(dec, triu, precision=lax.Precision.HIGHEST)
        cum_v[rows, :] = LOG2E * cum
        total = cum[BQ - 1 : BQ]
        totals.append(total)
        ecx_v[rows, :] = high_low(jnp.exp(cum))
        rem_v[rows, :] = high_low(jnp.exp(total - cum) * valid[rows])
        bt_v[:, rows] = b_ref[rows, :].astype(F32).T.astype(BF16)
        g = dot(c_ref[rows, :], b_ref[rows, :], ((1,), (1,)))
        g_v[k] = g * tri
    row = iota((16, HEADS), 0)
    small = jnp.where(row == 3, jnp.exp(totals[0] + totals[1] + totals[2]), jnp.where(row == 4, dsk_ref[...], 0.0))
    for k in range(NCH):
        small = jnp.where(row == k, jnp.exp(totals[k]), small)
    thr_v[...] = dot(high_low(small), e2_v[...])

    each_peer(lambda d: tab_from(d).wait_recv())
    to_tab = pltpu.make_async_copy(rtab_v, rtab_s, load_sem.at[8])
    to_tab.start()
    to_tab.wait()
    to_pos.wait()
    loads[0].wait()

    def pack_state(i, _):
        for c in range(CAP):
            sst[i * CAP + c] = stq[jnp.clip(rtab_s[i, 0, CAP + c], 0, 63)]
        return 0

    lax.fori_loop(0, OWN, pack_state, 0)
    each_peer(lambda d: st_copy(d, True).start())
    loads[1].wait()
    for part in range(2):
        def pack_kv(i, _, part=part):
            for c in range(CAP):
                skv[part, i * CAP + c] = kvq[jnp.clip(rtab_s[i, 0, c], 0, 31), part]
            return 0

        lax.fori_loop(0, OWN, pack_kv, 0)
        each_peer(lambda d, part=part: kv_copy(part, d, True).start())
    for c in range(CAP):
        rst[b * CAP + c] = sst[b * CAP + c]
        for part in range(2):
            arrived[part][b * CAP + c] = skv[part, b * CAP + c]

    loads[4].wait()

    def end_tile(j, _):
        lanes = pl.ds(pl.multiple_of(j * LT, LT), LT)
        total = None
        for k in range(NCH):
            rows = slice(k * BQ, (k + 1) * BQ)
            xr = (x_v[rows, lanes].astype(F32) * dot(rem_v[rows, :], e2_v[:, lanes])).astype(BF16)
            part = dot(bt_v[:, rows], xr)
            if k < NCH - 1:
                l_v[k, :, lanes] = part
            total = part if k == 0 else thr_v[k : k + 1, lanes] * total + part
        lend_v[:, lanes] = total
        return 0

    lax.fori_loop(0, CH // LT, end_tile, 0)

    each_peer(lambda d: st_copy(d, False).wait_recv())

    def place(j, _):
        sta[pl.ds(pl.multiple_of(j * 16, 16), 16), :] = rst[jnp.clip(pos_s[1, j], 0, OWN * CAP - 1)]
        return 0

    lax.fori_loop(0, ENT, place, 0)
    r, c = iota((KEYS, KEYS), 0), iota((KEYS, KEYS), 1)
    order = jnp.where(c == ((r >> 1) & 7) * 64 + (r >> 4) * 2 + (r & 1), 1.0, 0.0).astype(BF16)
    sts[...] = dot(sta[...], order, ((0,), (0,))).astype(BF16)

    def sx_copy(q):
        return pltpu.make_async_remote_copy(
            src_ref=sts, dst_ref=inc.at[q], send_sem=sx_sem.at[0, 0], recv_sem=sx_sem.at[1, q],
            device_id=(0, b, m), device_id_type=MESH)

    @pl.when(s == 0)
    def _():
        inc[0] = sts[...]

    @pl.when(s > 0)
    def _():
        sx_copy(s).start()

    first = iota((BQ, BQ), 1) < 64

    def within(k, _):
        rows = pl.ds(pl.multiple_of(k * BQ, BQ), BQ)
        cum = cum_v[rows, :]
        cumt = cumt_v[pl.ds(pl.multiple_of(k * HEADS, HEADS), HEADS), :]
        g = g_v[k]
        for j in range(HEADS // 2):
            lanes = slice(j * 128, (j + 1) * 128)
            sides = []
            for h in (2 * j, 2 * j + 1):
                spread = cum[:, h : h + 1] - cumt[h : h + 1, :]
                sides.append((jnp.exp2(jnp.minimum(spread, 0.0)) * g).astype(BF16))
            xp = x_v[rows, lanes]
            zero = jnp.zeros_like(xp)
            both = jnp.concatenate([jnp.where(first, xp, zero), jnp.where(first, zero, xp)], axis=0)
            y_v[rows, lanes] = dot(jnp.concatenate(sides, axis=1), both)
        return 0

    lax.fori_loop(0, NCH, within, 0)

    def ag_copy(i, part, q, to):
        return pltpu.make_async_remote_copy(
            src_ref=kvall.at[q, part], dst_ref=kvall.at[q, part], send_sem=ag_sem.at[0, i], recv_sem=ag_sem.at[1, i],
            device_id=(to, b, m), device_id_type=MESH)

    def put_in_order(part):
        each_peer(lambda d: kv_copy(part, d, False).wait_recv())
        nothing = jnp.zeros((16, 2 * HD), BF16)

        def in_order(e, _):
            to = pl.ds(pl.multiple_of(e * 16, 16), 16)
            listed = e < cached[0]
            place_of = pos_s[0, e] if part else jnp.where(listed, pos_s[0, e], pos_s[0, 0])
            rows = arrived[part][jnp.clip(place_of, 0, OWN * CAP - 1)]
            kvall[s, part, to, :] = jnp.where(listed, rows, nothing) if part else rows
            return 0

        lax.fori_loop(0, ENT, in_order, 0)
        ag_copy(part, part, s, right).start()
        ag_copy(2 + part, part, s, left).start()

    def ch_copy(g):
        return pltpu.make_async_remote_copy(
            src_ref=snd.at[g], dst_ref=inc.at[g], send_sem=ch_sem.at[0, g], recv_sem=ch_sem.at[1, g],
            device_id=(lax.rem(s + 1, SEQ), b, m), device_id_type=MESH)

    def chain(who):
        @pl.when(s == who)
        def _():
            for g in range(SEQ):
                lanes = slice(g * KEYS, (g + 1) * KEYS)
                if who == 0 and g > 0:
                    sx_copy(g).wait_recv()
                if who > 0:
                    ch_copy(g).wait_recv()
                if who < SEQ - 1:
                    snd[g] = (thr_v[3:4, lanes] * inc[g].astype(F32) + lend_v[:, lanes]).astype(BF16)
                    ch_copy(g).start()

    loads[5].wait()
    for h in range(QH):
        qs_v[h] = high_low(q_v[:, h * HD : (h + 1) * HD].astype(F32) * SCALE2)
    m_v[...] = jnp.full(m_v.shape, NEGATIVE, F32)
    acc_v[...] = jnp.zeros(acc_v.shape, F32)

    def attend(key_ref, value_ref, change, weigh, more=None):
        def group(g, _):
            shared = pl.ds(pl.multiple_of(g * HD, HD), HD)
            keys = key_ref[:, shared]
            if more is not None:
                keys = jnp.concatenate([keys, more[0][:, shared]], axis=0)
            keys = jnp.concatenate([keys, keys], axis=1)
            values = value_ref[:, shared]
            values = jnp.concatenate([values, jnp.ones_like(values) if weigh is None else weigh[...]], axis=1)
            if more is not None:
                values = jnp.concatenate([values, jnp.concatenate([more[1][:, shared], weigh[...]], axis=1)], axis=0)
            for i in range(4):
                scores = dot(qs_v[4 * g + i], keys, ((1,), (1,)))
                if change is not None:
                    scores = change(scores)
                before = m_v[g, i]
                now = jnp.maximum(before, jnp.max(scores, axis=1, keepdims=True))
                m_v[g, i] = now
                width = scores.shape[1] // 128
                probs = jnp.exp2(scores - jnp.concatenate([now] * width, axis=1)).astype(BF16)
                shrink = jnp.exp2(before - now)
                acc_v[g, i] = acc_v[g, i] * jnp.concatenate([shrink, shrink], axis=1) + dot(probs, values)
            return 0

        lax.fori_loop(0, QH // 4, group, 0, unroll=2)

    def causal(scores):
        return jnp.where(iota((T, T), 1) <= iota((T, T), 0), scores, NEGATIVE)

    nk_arrive(1, 1, 1)
    nk_arrive(0, 0, 1)
    for hop in onward:
        nk_send(*hop)
    weigh_v[...] = jnp.where(iota((KEYS, HD), 0) < cached[0] * 16, 1.0, 0.0).astype(BF16)
    chain(0)
    put_in_order(0)
    chain(1)
    attend(nkv.at[s, 0], nkv.at[s, 1], causal, None)
    put_in_order(1)
    chain(2)
    ag_copy(0, 0, left, right).wait_recv()
    ag_copy(4, 0, left, right).start()
    attend(kvall.at[s, 0], kvall.at[s, 1], None, weigh_v)
    ag_copy(3, 1, right, left).wait_recv()
    ag_copy(5, 1, right, left).start()
    for hop in hops[:3] + onward:
        nk_arrive(*hop)

    def earlier(j, _):
        attend(nkv.at[j, 0], nkv.at[j, 1], None, None)
        return 0

    lax.fori_loop(0, s, earlier, 0)
    ag_copy(2, 0, right, left).wait_recv()
    ag_copy(1, 1, left, right).wait_recv()
    attend(kvall.at[left, 0], kvall.at[left, 1], None, weigh_v, (kvall.at[right, 0], kvall.at[right, 1]))
    chain(3)

    loads[6].wait()

    def gate_tile(j, sums):
        lanes = pl.ds(pl.multiple_of(j * LT, LT), LT)
        state = inc[j // 2, :, pl.ds(pl.multiple_of((j % 2) * LT, LT), LT)].astype(F32)
        out = []
        for k in range(NCH):
            rows = slice(k * BQ, (k + 1) * BQ)
            carried = dot(c_ref[rows, :], state.astype(BF16)) * dot(ecx_v[rows, :], e2_v[:, lanes])
            y = y_v[rows, lanes] + carried + thr_v[4:5, lanes] * x_v[rows, lanes].astype(F32)
            z = z_v[rows, lanes].astype(F32)
            gated = y * (z / (1.0 + jnp.exp(-z)))
            y_v[rows, lanes] = gated
            square = gated * gated
            out.append(sums[k] + square[:, :128] + square[:, 128:])
            if k < NCH - 1:
                state = thr_v[k : k + 1, lanes] * state + l_v[k, :, lanes]
        return tuple(out)

    sums = lax.fori_loop(0, CH // LT, gate_tile, tuple(jnp.zeros((BQ, 128), F32) for _ in range(NCH)))
    ssx[m] = jnp.zeros((8, 128), F32)
    for k in range(NCH):
        ssx[m, k : k + 1, :] = jnp.sum(sums[k].T, axis=0, keepdims=True)

    def mp_copy(d, to):
        other = lax.rem(m + d, MPS) if to else lax.rem(m + MPS - d, MPS)
        at = m if to else other
        return pltpu.make_async_remote_copy(
            src_ref=ssx.at[at], dst_ref=ssx.at[at], send_sem=mp_sem.at[0, d], recv_sem=mp_sem.at[1, d],
            device_id=(s, b, other), device_id_type=MESH)

    for d in range(1, MPS):
        mp_copy(d, True).start()

    ag_copy(4, 0, across, right).wait_recv()
    ag_copy(5, 1, across, left).wait_recv()
    attend(kvall.at[across, 0], kvall.at[across, 1], None, weigh_v)

    def attn_out(h, _):
        at = pl.ds(pl.multiple_of(h * HD, HD), HD)
        both = acc_v[h // 4, h % 4]
        attn_ref[:, at] = (both[:, :HD] / both[:, HD:] * valid).astype(BF16)
        return 0

    lax.fori_loop(0, QH, attn_out, 0)

    for d in range(1, MPS):
        mp_copy(d, False).wait_recv()
    whole = ssx[0] + ssx[1] + ssx[2] + ssx[3]
    factor = lax.rsqrt(whole / (HEADS * 64 * MPS) + EPSILON)
    for k in range(NCH):
        rows = slice(k * BQ, (k + 1) * BQ)
        scale = jnp.broadcast_to(factor[k : k + 1], (BQ, BQ)).T * valid[rows]

        def norm_tile(j, _, rows=rows, scale=scale):
            lanes = pl.ds(pl.multiple_of(j * LT, LT), LT)
            ssm_ref[rows, lanes] = (y_v[rows, lanes] * jnp.concatenate([scale, scale], axis=1) * gain_ref[:, lanes]).astype(BF16)
            return 0

        lax.fori_loop(0, CH // LT, norm_tile, 0)

    each_peer(lambda d: tab_copy(d).wait_send())
    each_peer(lambda d: st_copy(d, True).wait_send())
    for part in range(2):
        each_peer(lambda d, part=part: kv_copy(part, d, True).wait_send())
    for who, slot, way in hops + onward:
        @pl.when(s == who)
        def _(slot=slot, way=way):
            nk_copy(slot, way).wait_send()

    @pl.when(s > 0)
    def _():
        sx_copy(s).wait_send()

    for part in range(2):
        ag_copy(part, part, s, right).wait_send()
        ag_copy(2 + part, part, s, left).wait_send()
    ag_copy(4, 0, left, right).wait_send()
    ag_copy(5, 1, right, left).wait_send()

    @pl.when(s < SEQ - 1)
    def _():
        for g in range(SEQ):
            ch_copy(g).wait_send()

    for d in range(1, MPS):
        mp_copy(d, True).wait_send()


def per_device(
    xs, gate_z, b_in, c_in, log_decay, d_skip, norm_gain, queries, keys_new, values_new,
    kv_pool, state_pool, new_len, cached_blocks, kv_owner, kv_slot, state_owner, state_slot,
):
    pieces = state_pool.reshape(state_pool.shape[0], 2 * HEADS, NS)
    vmem, smem = pl.BlockSpec(memory_space=pltpu.VMEM), pl.BlockSpec(memory_space=pltpu.SMEM)
    hbm = pl.BlockSpec(memory_space=pltpu.HBM)
    scratch = [
        pltpu.VMEM((T, CH), BF16),
        pltpu.VMEM((T, CH), BF16),
        pltpu.VMEM((T, QH * HD), BF16),
        pltpu.VMEM((SEQ, 2, T, 2 * HD), BF16),
        pltpu.VMEM((32, 2, 16, 2 * HD), BF16),
        pltpu.VMEM((64, 16, NS), BF16),
        pltpu.VMEM((OWN, 1, 128), I32),
        pltpu.VMEM((OWN, 1, 128), I32),
        pltpu.VMEM((8, 128), I32),
        pltpu.SMEM((OWN, 1, 128), I32),
        pltpu.SMEM((8, 128), I32),
        pltpu.VMEM((2, OWN * CAP, 16, 2 * HD), BF16),
        pltpu.VMEM((OWN * CAP, 16, 2 * HD), BF16),
        pltpu.VMEM((OWN * CAP, 16, 2 * HD), BF16),
        pltpu.VMEM((SEQ, 2, KEYS, 2 * HD), BF16),
        pltpu.VMEM((OWN * CAP, 16, NS), BF16),
        pltpu.VMEM((OWN * CAP, 16, NS), BF16),
        pltpu.VMEM((KEYS, NS), BF16),
        pltpu.VMEM((NS, KEYS), BF16),
        pltpu.VMEM((SEQ, NS, KEYS), BF16),
        pltpu.VMEM((SEQ, NS, KEYS), BF16),
        pltpu.VMEM((MPS, 8, 128), F32),
        pltpu.VMEM((T, HEADS), F32),
        pltpu.VMEM((NCH * HEADS, BQ), F32),
        pltpu.VMEM((T, 2 * HEADS), BF16),
        pltpu.VMEM((2 * HEADS, CH), BF16),
        pltpu.VMEM((16, CH), F32),
        pltpu.VMEM((NCH, BQ, BQ), F32),
        pltpu.VMEM((NS, T), BF16),
        pltpu.VMEM((T, 2 * HEADS), BF16),
        pltpu.VMEM((NCH - 1, NS, CH), F32),
        pltpu.VMEM((NS, CH), F32),
        pltpu.VMEM((T, CH), F32),
        pltpu.VMEM((QH, T, 2 * HD), BF16),
        pltpu.VMEM((KEYS, HD), BF16),
        pltpu.VMEM((2, QH // 2, T, 128), F32),
        pltpu.VMEM((2, QH // 2, T, 2 * HD), F32),
        pltpu.SemaphoreType.DMA((9,)),
        pltpu.SemaphoreType.DMA((2, OWN)),
        pltpu.SemaphoreType.DMA((2, 2, OWN)),
        pltpu.SemaphoreType.DMA((2, OWN)),
        pltpu.SemaphoreType.DMA((2, 6)),
        pltpu.SemaphoreType.DMA((2, SEQ, 2)),
        pltpu.SemaphoreType.DMA((2, SEQ)),
        pltpu.SemaphoreType.DMA((2, SEQ)),
        pltpu.SemaphoreType.DMA((2, MPS)),
    ]
    ssm, attn = pl.pallas_call(
        kernel,
        name="prefill",
        out_shape=(jax.ShapeDtypeStruct((T, CH), BF16), jax.ShapeDtypeStruct((T, QH * HD), BF16)),
        in_specs=[smem, smem] + [vmem] * 9 + [hbm] * 7,
        out_specs=(vmem, vmem),
        scratch_shapes=scratch,
        compiler_params=pltpu.CompilerParams(
            collective_id=0, has_side_effects=True, vmem_limit_bytes=44 * 1024 * 1024),
    )(
        new_len, cached_blocks,
        *(pltpu.with_memory_space_constraint(value, pltpu.HBM) for value in (
            kv_owner[:, :, 0], kv_slot, state_owner[:, :, 0], state_slot,
            b_in[0], c_in[0], log_decay[0].T, d_skip.reshape(1, HEADS), norm_gain.reshape(1, CH),
            xs[0], gate_z[0], queries[0], keys_new[0], values_new[0], kv_pool, pieces,
        )),
    )
    return (ssm[None], attn[None])


def solution(mesh):
    in_specs = (
        P("batch", "seq", "mp"),
        P("batch", "seq", "mp"),
        P("batch", "seq", None),
        P("batch", "seq", None),
        P("batch", "seq", "mp"),
        P("mp"),
        P("mp"),
        P("batch", "seq", "mp"),
        P("batch", "seq", "mp"),
        P("batch", "seq", "mp"),
        P("batch", None, None, "mp"),
        P("batch", "mp", None, None),
        P("batch"),
        P("batch"),
        P("batch", None, None),
        P("batch", None),
        P("batch", None, None),
        P("batch", None),
    )
    out_specs = (P("batch", "seq", "mp"), P("batch", "seq", "mp"))
    return jax.shard_map(
        per_device, mesh=mesh, in_specs=in_specs, out_specs=out_specs, check_vma=False
    )
```
